32 devices in a mesh: seq: 32 (over z, y, x, core).
Axes of the slice: x: 2, y: 2, z: 4, core: 2. Of those that a mesh axis runs over, the one named last changes fastest.
Arguments:
- layer_input: float32 [4096, 1024], P('seq'), may hold values from -6 to 6
- out_grad: float32 [4096, 1024], P('seq'), may hold values from -6 to 6
- doc_ids: int32 [4096], replicated, may hold values from 0 to 23, never falling along the last dimension, each value on 1 to 2176 neighbouring positions
- norm1_gain: bfloat16 [1024], P('seq'), may hold values from 0.5 to 1.5
- in_weight: bfloat16 [1024, 3352], P('seq'), may hold values from -0.1875 to 0.1875
- conv_weight: float32 [4, 1792], replicated, may hold values from -3 to 3
- conv_bias: float32 [1792], replicated, may hold values from -3 to 3
- dt_bias: float32 [24], replicated, may hold values from -4.5 to -1.5
- decay_log: float32 [24], replicated, may hold values from -7 to -1
- skip_gain: float32 [24], replicated, may hold values from 0.5 to 1.5
- mixer_out: bfloat16 [1536, 1024], P(None, 'seq'), may hold values from -0.15625 to 0.15625
- query_weight: bfloat16 [1024, 512], P('seq'), may hold values from -0.1875 to 0.1875
- keyvalue_weight: bfloat16 [1024, 256], P('seq'), may hold values from -0.1875 to 0.1875
- attn_out: bfloat16 [512, 1024], P(None, 'seq'), may hold values from -2 to 2
- norm2_gain: bfloat16 [1024], P('seq'), may hold values from 0.5 to 1.5
- gate_up: bfloat16 [1024, 4096], P('seq'), may hold values from -0.1875 to 0.1875
- down_weight: bfloat16 [2048, 1024], P(None, 'seq'), may hold values from -0.125 to 0.125
Outputs:
- layer_output: float32 [4096, 1024], P('seq')
- input_grad: float32 [4096, 1024], P('seq')
- norm1_gain_grad: float32 [1024], P('seq')
- in_weight_grad: float32 [1024, 3352], P('seq')
- conv_weight_grad: float32 [4, 1792], replicated
- conv_bias_grad: float32 [1792], replicated
- dt_bias_grad: float32 [24], replicated
- decay_log_grad: float32 [24], replicated
- skip_gain_grad: float32 [24], replicated
- mixer_out_grad: float32 [1536, 1024], P(None, 'seq')
- query_weight_grad: float32 [1024, 512], P('seq')
- keyval_weight_grad: float32 [1024, 256], P('seq')
- attn_out_grad: float32 [512, 1024], P(None, 'seq')
- norm2_gain_grad: float32 [1024], P('seq')
- gate_up_grad: float32 [1024, 4096], P('seq')
- down_weight_grad: float32 [2048, 1024], P(None, 'seq')
The draws below stay inside these ranges and needn't reach their ends.
Inputs may be any that keep to these rules, and one draw needn't show every extreme that they name: doc_ids never decreases along the sequence; each document is a run of 1 to 2176 positions, and one has exactly 2176.
All inputs are finite; a program needn't handle non-finite values.
Results may differ from the reference program's by a relative error of at most 0.013.
Values may be sent and summed in bfloat16 or wider, within the bound.
No kernel may reach another device: no remote copies, remote signals or barrier semaphores. Data moves between devices by JAX's collectives and lax.ppermute only.
A program may use at most 320 MiB of HBM per device.

```python
import math
from functools import partial
import jax
import jax.numpy as jnp
import numpy as np
from jax import lax

MODEL_WIDTH = 1024
FF = 2048
HM = 24
HP = 64
NS = 128
KC = 4
QUERY_HEADS = 8
KEYVALUE_HEADS = 2
HEAD_SIZE = 64
SPAN = 128
DOCS = 24
SEQ = 4096
DOC_MOST = 2176
DSSM = 1536
CONV_CH = 1792
PROJ = 3352


def strengthened(values, stream_key, source, target, shards_of, factor):
    def block_of(dim):
        return (jnp.arange(values.shape[dim]) // (values.shape[dim] // shards_of)).reshape((-1,) + (1,) * (values.ndim - 1 - dim))

    first = jax.random.permutation(stream_key, shards_of)[block_of(target)]
    second = (block_of(target) + shards_of // 2) % shards_of
    return jnp.where((block_of(source) == first) | (block_of(source) == second), factor * values, values)


def block_scale(stream_key, dims, shards, smallest, largest):
    loudness, own = 1.0, jax.random.fold_in(stream_key, 6)
    for dim, shards_of in shards:
        draws = jnp.exp(jax.random.uniform(jax.random.fold_in(own, dim), (shards_of,), jnp.float32, smallest / len(shards), largest / len(shards)))
        loudness = loudness * jnp.repeat(draws, dims[dim] // shards_of).reshape([-1 if axis == dim else 1 for axis in range(len(dims))])
    return loudness


def length_profile(count, total, limit, slope):
    portions = [(1 << 20) // math.isqrt(grade ** slope) + 1 for grade in range(2, count + 1)]
    surplus, holding = total - limit - (count - 1), [1] * (count - 1)
    while surplus > 0:
        candidates = [i for i in range(count - 1) if holding[i] < limit]
        pool, remaining = sum([portions[i] for i in candidates]), surplus
        for i in candidates:
            more = min(limit - holding[i], max(1, remaining * portions[i] // pool), surplus)
            holding[i] = holding[i] + more
            surplus = surplus - more
    return np.array([limit] + holding)


def uneven(stream_key, count, total, most, skew):
    if count == 2:
        one = jax.random.randint(stream_key, (), max(1, total - most), min(most, total - 1) + 1)
        return jnp.stack([one, total - one])
    sizes = jnp.asarray(length_profile(count, total, most, skew), jnp.int32)
    couples = (count - 1) // 2
    donor, sink = sizes[1:1 + 2 * couples:2], sizes[2:2 + 2 * couples:2]
    slack = jnp.minimum(donor - 1, most - sink)
    shifted = jax.random.randint(jax.random.fold_in(stream_key, 1), (couples,), 0, 1 << 20) % (slack + 1)
    sizes = sizes.at[1:1 + 2 * couples:2].set(donor - shifted).at[2:2 + 2 * couples:2].set(sink + shifted)
    return sizes[jax.random.permutation(jax.random.fold_in(stream_key, 2), count)]


def centred(stream_key, shape, scale, bound, shards=(), held_as=jnp.bfloat16):
    factor_of = block_scale(stream_key, shape, shards, -0.22, 0.18) if shards else 1.0
    result = jax.random.normal(stream_key, shape, jnp.float32) * scale * factor_of
    return jnp.minimum(jnp.maximum(result, -bound), bound).astype(held_as)


def gaussian_with(stream_key, shape, spread, bound, cuts, heavy, held_as=jnp.bfloat16):
    drawn = spread * jax.random.normal(stream_key, shape, jnp.float32)
    if cuts:
        drawn = drawn * block_scale(stream_key, shape, cuts, -0.22, 0.18)
    return jnp.clip(strengthened(drawn, jax.random.fold_in(stream_key, 3), *heavy), -bound, bound).astype(held_as)


def setup_inputs(seed: int = 0) -> dict:
    key_of = jax.random.split(jax.random.key(seed), 18)
    return {
        "layer_input": gaussian_with(key_of[0], (SEQ, MODEL_WIDTH), 1.0, 6.0, ((0, 32),), (0, 1, 32, 2.75), jnp.float32),
        "out_grad": gaussian_with(key_of[1], (SEQ, MODEL_WIDTH), 1.0, 6.0, ((0, 32),), (0, 1, 32, 2.75), jnp.float32),
        "doc_ids": jnp.searchsorted(jnp.cumsum(uneven(key_of[2], DOCS, SEQ, DOC_MOST, 0)), jnp.arange(SEQ), side="right").astype(jnp.int32),
        "norm1_gain": jnp.clip(1.0 + 0.1 * jax.random.normal(key_of[3], (MODEL_WIDTH,), jnp.float32), 0.5, 1.5).astype(jnp.bfloat16),
        "in_weight": centred(key_of[4], (MODEL_WIDTH, PROJ), MODEL_WIDTH ** -0.5, 0.1875, ((0, 32),)),
        "conv_weight": centred(key_of[5], (KC, CONV_CH), KC ** -0.5, 3.0, (), jnp.float32),
        "conv_bias": centred(key_of[6], (CONV_CH,), 0.5, 3.0, (), jnp.float32),
        "dt_bias": jnp.clip(jax.random.uniform(key_of[7], (HM,), jnp.float32, -4.5, -1.5), -4.5, -1.5),
        "decay_log": jnp.clip(jax.random.uniform(key_of[8], (HM,), jnp.float32, -7.0, -1.0), -7.0, -1.0),
        "skip_gain": jnp.clip(jax.random.uniform(key_of[9], (HM,), jnp.float32, 0.5, 1.5), 0.5, 1.5),
        "mixer_out": centred(key_of[10], (DSSM, MODEL_WIDTH), DSSM ** -0.5, 0.15625, ((1, 32),)),
        "query_weight": centred(key_of[11], (MODEL_WIDTH, QUERY_HEADS * HEAD_SIZE), MODEL_WIDTH ** -0.5, 0.1875, ((0, 32),)),
        "keyvalue_weight": centred(key_of[12], (MODEL_WIDTH, 2 * KEYVALUE_HEADS * HEAD_SIZE), MODEL_WIDTH ** -0.5, 0.1875, ((0, 32),)),
        "attn_out": centred(key_of[13], (QUERY_HEADS * HEAD_SIZE, MODEL_WIDTH), 8 ** -0.5, 2.0, ((1, 32),)),
        "norm2_gain": jnp.clip(1.0 + 0.1 * jax.random.normal(key_of[14], (MODEL_WIDTH,), jnp.float32), 0.5, 1.5).astype(jnp.bfloat16),
        "gate_up": centred(key_of[15], (MODEL_WIDTH, 2 * FF), MODEL_WIDTH ** -0.5, 0.1875, ((0, 32),)),
        "down_weight": centred(key_of[16], (FF, MODEL_WIDTH), FF ** -0.5, 0.125, ((1, 32),)),
    }


EPS = 1e-05
HIGH = lax.Precision.HIGHEST
NEG = -1e+30

def matmul(left, right):
    return jnp.dot(left, right, preferred_element_type=jnp.float32)

def matmul_tn(left, right):
    return lax.dot_general(left, right, (((0,), (0,)), ((), ())), preferred_element_type=jnp.float32)

def matmul_nt(left, right):
    return lax.dot_general(left, right, (((1,), (1,)), ((), ())), preferred_element_type=jnp.float32)

def rms_scale(values):
    return lax.rsqrt(lax.optimization_barrier(jnp.mean(values * values, axis=-1, keepdims=True)) + EPS)

def rms_back(values, inverse, gain_row, upstream):
    scaled = upstream * gain_row
    return inverse * (scaled - values * inverse * inverse * lax.optimization_barrier(jnp.mean(scaled * values, axis=-1, keepdims=True)))

def silu_slope(values):
    logistic = jax.nn.sigmoid(values)
    return logistic * (1.0 + values * (1.0 - logistic))

def conv_apply(seg_window, conv_ext, conv_weight, conv_bias):
    out_rows = conv_ext.shape[0] - (KC - 1)
    summed = jnp.broadcast_to(conv_bias[None, :], (out_rows, conv_ext.shape[1]))
    for offset in range(KC):
        same_doc = seg_window[offset:offset + out_rows] == seg_window[KC - 1:]
        summed = summed + conv_weight[offset][None, :] * jnp.where(same_doc[:, None], conv_ext[offset:offset + out_rows], 0.0)
    return jax.nn.silu(summed)

def ssm_core(seg_here, seg_before, conv_act, dt_raw, dt_bias, decay_log, skip_gain):
    row_count = conv_act.shape[0]
    blocks_count = row_count // SPAN
    ssm_x = conv_act[:, :HM * HP].reshape(blocks_count, SPAN, HM, HP)
    ssm_b = conv_act[:, HM * HP:HM * HP + NS].reshape(blocks_count, SPAN, NS)
    ssm_c = conv_act[:, HM * HP + NS:].reshape(blocks_count, SPAN, NS)
    step_size = jax.nn.softplus(dt_raw + dt_bias[None, :])
    log_decay = -jnp.exp(decay_log)[None, :] * step_size
    step_heads = step_size.reshape(blocks_count, SPAN, HM).transpose(0, 2, 1)
    cumulative = jnp.cumsum(log_decay.reshape(blocks_count, SPAN, HM).transpose(0, 2, 1), axis=2)
    seg_blocks = seg_here.reshape(blocks_count, SPAN)
    seg_prior = jnp.concatenate([jnp.reshape(seg_before, (1,)).astype(jnp.int32), seg_blocks[:-1, -1].astype(jnp.int32)])
    seg_last = seg_blocks[:, -1]
    lower = jnp.arange(SPAN)[:, None] >= jnp.arange(SPAN)[None, :]
    visible = (lower[None] & (seg_blocks[:, :, None] == seg_blocks[:, None, :]))[:, None]
    gaps = cumulative[:, :, :, None] - cumulative[:, :, None, :]
    mixing = jnp.where(visible, jnp.exp(jnp.where(visible, gaps, 0.0)), 0.0)
    inner = jnp.einsum('ktn,ksn->kts', ssm_c, ssm_b, precision=HIGH)
    weighted = mixing * inner[:, None] * step_heads[:, :, None, :]
    intra = jnp.einsum('khts,kshp->kthp', weighted, ssm_x, precision=HIGH)
    to_end = jnp.where((seg_blocks == seg_last[:, None])[:, None, :], jnp.exp(cumulative[:, :, -1:] - cumulative), 0.0) * step_heads
    block_states = jnp.einsum('khs,kshp,ksn->khpn', to_end, ssm_x, ssm_b, precision=HIGH)
    from_start = jnp.where((seg_blocks == seg_prior[:, None])[:, None, :], jnp.exp(cumulative), 0.0)
    block_decay = from_start[:, :, -1]

    def advance(carried, inputs):
        state_now, product = carried
        decay_now, fresh = inputs
        return ((decay_now[:, None, None] * state_now + fresh, product * decay_now), (state_now, product))
    initial_carry = (jnp.zeros((HM, HP, NS), jnp.float32), jnp.ones((HM,), jnp.float32))
    (final_state, unused), (entering, products) = lax.scan(advance, initial_carry, (block_decay, block_states))
    carried_in = jnp.einsum('kht,ktn,khpn->kthp', from_start, ssm_c, entering, precision=HIGH)
    local_out = (intra + carried_in + skip_gain[None, None, :, None] * ssm_x).reshape(row_count, HM, HP)
    reach = (from_start * products[:, :, None]).transpose(1, 0, 2).reshape(HM, row_count)
    return (local_out, final_state, reach, ssm_c.reshape(row_count, NS))

def over_keys(update, initial_carry, key_rows_all, first_key, row_limit, query_rows, doc_span):
    count_all = key_rows_all.shape[0]
    block_size = math.gcd(count_all, 512)
    blocks = count_all // block_size
    visits = min(blocks, (doc_span + query_rows - 1) // block_size + 2)
    lowest = (row_limit - query_rows - doc_span + 1 - first_key) // block_size
    begin = jnp.clip(lowest, 0, blocks - visits).astype(jnp.int32)

    def visit(number, current_block):
        offset = ((begin + number) * block_size).astype(jnp.int32)
        return update(current_block, lax.dynamic_slice_in_dim(key_rows_all, offset, block_size, 0), (first_key + offset).astype(jnp.int32))
    return lax.fori_loop(0, visits, visit, initial_carry)

def block_scores(query_quadruple, positions, seg_rows, doc_ids, block_forward_pass, key_start):
    rows_per_block = block_forward_pass.shape[0]
    key_columns = KEYVALUE_HEADS * HEAD_SIZE
    key_row_block = block_forward_pass[:, :key_columns].reshape(rows_per_block, KEYVALUE_HEADS, HEAD_SIZE)
    value_row_block = block_forward_pass[:, key_columns:].reshape(rows_per_block, KEYVALUE_HEADS, HEAD_SIZE)
    key_pos = key_start + jnp.arange(rows_per_block, dtype=jnp.int32)
    key_seg = lax.dynamic_slice_in_dim(doc_ids, key_start, rows_per_block)
    visible = (key_pos[None, :] <= positions[:, None]) & (key_seg[None, :] == seg_rows[:, None])
    attention_scores = jnp.einsum('uoiy,woy->oiuw', query_quadruple, key_row_block, preferred_element_type=jnp.float32) * HEAD_SIZE ** (-0.5)
    return (key_row_block, value_row_block, visible[None, None], attention_scores)

def stats_step(query_quadruple, positions, seg_rows, doc_ids, denominator, block_forward_pass, key_start):
    key_row_block, value_row_block, visible, attention_scores = block_scores(query_quadruple, positions, seg_rows, doc_ids, block_forward_pass, key_start)
    return denominator + lax.optimization_barrier(jnp.sum(jnp.exp(jnp.where(visible, attention_scores, NEG)), axis=3))

def values_step(query_quadruple, positions, seg_rows, doc_ids, log_total, current_block, block_forward_pass, key_start):
    key_row_block, value_row_block, visible, attention_scores = block_scores(query_quadruple, positions, seg_rows, doc_ids, block_forward_pass, key_start)
    attention_weights_soft = jnp.exp(jnp.where(visible, attention_scores - log_total[..., None], NEG)).astype(jnp.bfloat16)
    return current_block + jnp.einsum('zilr,rzq->lziq', attention_weights_soft, value_row_block, preferred_element_type=jnp.float32)

def back_step(query_quadruple, positions, seg_rows, doc_ids, log_total, gradient_quadruple, row_delta, current_block, block_forward_pass, key_start):
    query_accumulator, keyvalue_accumulator = current_block
    key_row_block, value_row_block, visible, attention_scores = block_scores(query_quadruple, positions, seg_rows, doc_ids, block_forward_pass, key_start)
    attention_weights_soft = jnp.exp(jnp.where(visible, attention_scores - log_total[..., None], NEG))
    probability_gradient = jnp.einsum('uoiy,woy->oiuw', gradient_quadruple, value_row_block, preferred_element_type=jnp.float32)
    score_gradient = (attention_weights_soft * (probability_gradient - row_delta[..., None])).astype(jnp.bfloat16)
    query_accumulator = query_accumulator + jnp.einsum('zilr,rzq->lziq', score_gradient, key_row_block, preferred_element_type=jnp.float32)
    key_portion = jnp.einsum('luzn,zlup->nlp', score_gradient, query_quadruple, preferred_element_type=jnp.float32) * HEAD_SIZE ** (-0.5)
    value_portion = jnp.einsum('luzn,zlup->nlp', attention_weights_soft.astype(jnp.bfloat16), gradient_quadruple, preferred_element_type=jnp.float32)
    rows_per_block = block_forward_pass.shape[0]
    block_gradient_out = jnp.concatenate([key_portion.reshape(rows_per_block, KEYVALUE_HEADS * HEAD_SIZE), value_portion.reshape(rows_per_block, KEYVALUE_HEADS * HEAD_SIZE)], axis=1)
    old_rows = lax.dynamic_slice_in_dim(keyvalue_accumulator, key_start, rows_per_block, 0)
    keyvalue_accumulator = lax.dynamic_update_slice_in_dim(keyvalue_accumulator, old_rows + block_gradient_out, key_start, 0)
    return (query_accumulator, keyvalue_accumulator)

def reference(layer_input, out_grad, doc_ids, norm1_gain, in_weight, conv_weight, conv_bias, dt_bias, decay_log, skip_gain, mixer_out, query_weight, keyvalue_weight, attn_out, norm2_gain, gate_up, down_weight):
    sequence_total = layer_input.shape[0]
    query_group_width = QUERY_HEADS // KEYVALUE_HEADS
    gain_first = norm1_gain.astype(jnp.float32)
    gain_second = norm2_gain.astype(jnp.float32)
    scale_one = rms_scale(layer_input)
    normed_one = (layer_input * scale_one * gain_first).astype(jnp.bfloat16)
    projected = matmul(normed_one, in_weight)
    gate_mix = projected[:, :DSSM]
    conv_in = projected[:, DSSM:DSSM + CONV_CH]
    dt_raw = projected[:, DSSM + CONV_CH:]
    seg_window = jnp.concatenate([jnp.full((KC - 1,), -1, jnp.int32), doc_ids.astype(jnp.int32)])
    conv_ext = jnp.concatenate([jnp.zeros((KC - 1, CONV_CH), jnp.float32), conv_in])
    conv_act, conv_pull = jax.vjp(partial(conv_apply, seg_window), conv_ext, conv_weight, conv_bias)
    ssm_parts, ssm_pull = jax.vjp(partial(ssm_core, doc_ids, jnp.int32(-1)), conv_act, dt_raw, dt_bias, decay_log, skip_gain)
    ssm_out = ssm_parts[0].reshape(sequence_total, DSSM)
    gated = (ssm_out * jax.nn.silu(gate_mix)).astype(jnp.bfloat16)
    mixer_part = matmul(gated, mixer_out)
    query_reduced = matmul(normed_one, query_weight).astype(jnp.bfloat16)
    keyval_low = matmul(normed_one, keyvalue_weight).astype(jnp.bfloat16)
    query_row_block = math.gcd(sequence_total, 1024)
    block_count = sequence_total // query_row_block
    block_starts = jnp.arange(block_count, dtype=jnp.int32) * query_row_block

    def block_inputs(first_entry):
        query_quadruple = lax.dynamic_slice_in_dim(query_reduced, first_entry, query_row_block, 0).reshape(query_row_block, KEYVALUE_HEADS, query_group_width, HEAD_SIZE)
        positions = first_entry + jnp.arange(query_row_block, dtype=jnp.int32)
        seg_rows = lax.dynamic_slice_in_dim(doc_ids, first_entry, query_row_block)
        return (query_quadruple, positions, seg_rows)

    def forward_block(first_entry):
        query_quadruple, positions, seg_rows = block_inputs(first_entry)
        initial_carry = jnp.zeros((KEYVALUE_HEADS, query_group_width, query_row_block), jnp.float32)
        denominator = over_keys(partial(stats_step, query_quadruple, positions, seg_rows, doc_ids), initial_carry, keyval_low, jnp.int32(0), first_entry + query_row_block, query_row_block, DOC_MOST)
        log_total = jnp.log(denominator)
        middle_initial = jnp.zeros((query_row_block, KEYVALUE_HEADS, query_group_width, HEAD_SIZE), jnp.float32)
        attn_block = over_keys(partial(values_step, query_quadruple, positions, seg_rows, doc_ids, log_total), middle_initial, keyval_low, jnp.int32(0), first_entry + query_row_block, query_row_block, DOC_MOST)
        return (attn_block, log_total)
    attn_blocks, logsumexp_totals = lax.map(forward_block, block_starts)
    attention_middle = attn_blocks.reshape(sequence_total, QUERY_HEADS * HEAD_SIZE)
    attn_low = attention_middle.astype(jnp.bfloat16)
    attn_part = matmul(attn_low, attn_out)
    resid = layer_input + mixer_part + attn_part
    scale_two = rms_scale(resid)
    normed_two = (resid * scale_two * gain_second).astype(jnp.bfloat16)
    gateup = matmul(normed_two, gate_up)
    gate_part = gateup[:, :FF]
    up_part = gateup[:, FF:]
    act_low = (jax.nn.silu(gate_part) * up_part).astype(jnp.bfloat16)
    layer_output = resid + matmul(act_low, down_weight)
    grad_low = out_grad.astype(jnp.bfloat16)
    down_weight_grad = matmul_tn(act_low, grad_low)
    act_grad = matmul_nt(grad_low, down_weight)
    gateup_grad_low = jnp.concatenate([act_grad * up_part * silu_slope(gate_part), act_grad * jax.nn.silu(gate_part)], axis=1).astype(jnp.bfloat16)
    gate_up_grad = matmul_tn(normed_two, gateup_grad_low)
    normed_two_grad = matmul_nt(gateup_grad_low, gate_up)
    norm2_gain_grad = lax.optimization_barrier(jnp.sum(normed_two_grad * resid * scale_two, axis=0))
    resid_grad = out_grad + rms_back(resid, scale_two, gain_second, normed_two_grad)
    resid_low = resid_grad.astype(jnp.bfloat16)
    mixer_out_grad = matmul_tn(gated, resid_low)
    attn_out_grad = matmul_tn(attn_low, resid_low)
    gated_grad = matmul_nt(resid_low, mixer_out)
    attention_gradient = matmul_nt(resid_low, attn_out)
    attention_gradient_reduced = attention_gradient.astype(jnp.bfloat16)

    def block_backward_pass(keyvalue_accumulator, inputs):
        first_entry, log_total = inputs
        query_quadruple, positions, seg_rows = block_inputs(first_entry)
        gradient_quadruple = lax.dynamic_slice_in_dim(attention_gradient_reduced, first_entry, query_row_block, 0).reshape(query_row_block, KEYVALUE_HEADS, query_group_width, HEAD_SIZE)
        gradient_block_pass = lax.dynamic_slice_in_dim(attention_gradient, first_entry, query_row_block, 0).reshape(query_row_block, KEYVALUE_HEADS, query_group_width, HEAD_SIZE)
        middle_block = lax.dynamic_slice_in_dim(attention_middle, first_entry, query_row_block, 0).reshape(query_row_block, KEYVALUE_HEADS, query_group_width, HEAD_SIZE)
        row_delta = lax.optimization_barrier(jnp.sum(gradient_block_pass * middle_block, axis=3)).transpose(1, 2, 0)
        initial_carry = (jnp.zeros((query_row_block, KEYVALUE_HEADS, query_group_width, HEAD_SIZE), jnp.float32), keyvalue_accumulator)
        query_accumulator, keyvalue_accumulator = over_keys(partial(back_step, query_quadruple, positions, seg_rows, doc_ids, log_total, gradient_quadruple, row_delta), initial_carry, keyval_low, jnp.int32(0), first_entry + query_row_block, query_row_block, DOC_MOST)
        return (keyvalue_accumulator, query_accumulator)
    keyvalue_accumulator, query_accumulators = lax.scan(block_backward_pass, jnp.zeros((sequence_total, 2 * KEYVALUE_HEADS * HEAD_SIZE), jnp.float32), (block_starts, logsumexp_totals))
    query_grad_low = (query_accumulators.reshape(sequence_total, QUERY_HEADS * HEAD_SIZE) * HEAD_SIZE ** (-0.5)).astype(jnp.bfloat16)
    keyval_grad_low = keyvalue_accumulator.astype(jnp.bfloat16)
    query_weight_grad = matmul_tn(normed_one, query_grad_low)
    keyval_weight_grad = matmul_tn(normed_one, keyval_grad_low)
    ssm_grad = gated_grad * jax.nn.silu(gate_mix)
    gate_mix_grad = gated_grad * ssm_out * silu_slope(gate_mix)
    cotangent = (ssm_grad.reshape(sequence_total, HM, HP), jnp.zeros((HM, HP, NS), jnp.float32), jnp.zeros((HM, sequence_total), jnp.float32), jnp.zeros((sequence_total, NS), jnp.float32))
    act_grad_ssm, dt_raw_grad, dt_bias_grad, decay_log_grad, skip_gain_grad = ssm_pull(cotangent)
    ext_grad, conv_weight_grad, conv_bias_grad = conv_pull(act_grad_ssm)
    conv_in_grad = ext_grad[KC - 1:]
    proj_grad_low = jnp.concatenate([gate_mix_grad, conv_in_grad, dt_raw_grad], axis=1).astype(jnp.bfloat16)
    in_weight_grad = matmul_tn(normed_one, proj_grad_low)
    normed_one_grad = matmul_nt(proj_grad_low, in_weight) + matmul_nt(query_grad_low, query_weight) + matmul_nt(keyval_grad_low, keyvalue_weight)
    norm1_gain_grad = lax.optimization_barrier(jnp.sum(normed_one_grad * layer_input * scale_one, axis=0))
    input_grad = resid_grad + rms_back(layer_input, scale_one, gain_first, normed_one_grad)
    return (layer_output, input_grad, norm1_gain_grad, in_weight_grad, conv_weight_grad, conv_bias_grad, dt_bias_grad, decay_log_grad, skip_gain_grad, mixer_out_grad, query_weight_grad, keyval_weight_grad, attn_out_grad, norm2_gain_grad, gate_up_grad, down_weight_grad)
```

```python
from functools import partial
import math

import jax
import jax.numpy as jnp
from jax import lax
from jax.experimental import pallas as pl
from jax.experimental.pallas import tpu as pltpu
from jax.sharding import PartitionSpec as P

FF = 2048
HM = 24
HP = 64
NS = 128
KC = 4
QUERY_HEADS = 8
KEYVALUE_HEADS = 2
HEAD_SIZE = 64
SPAN = 128
DSSM = 1536
CONV_CH = 1792


EPS = 1e-05
HIGH = lax.Precision.HIGHEST
NEG = -1e30


def passed_along(block, axis, distance):
    devices = range(lax.axis_size(axis))
    route = [(i - distance, i) for i in devices if i - distance in devices]
    return lax.ppermute(block, axis, route)


def ring_order(devices):
    chips = devices // 2
    depth = 4
    side = math.isqrt(max(chips // depth, 1))
    if devices % 2 or chips != depth * side * side or side % 2:
        return list(range(devices))
    plane = []
    for a in range(side):
        line = [(a, b) for b in range(1, side)]
        plane += line if a % 2 == 0 else line[::-1]
    plane += [(a, 0) for a in range(side - 1, -1, -1)]
    order = []
    for number, (a, b) in enumerate(plane):
        levels = range(depth) if number % 2 == 0 else range(depth - 1, -1, -1)
        for z in levels:
            chip = (z * side + a) * side + b
            order += [2 * chip, 2 * chip + 1]
    return order


def reordered(values, order):
    width = values.shape[1] // len(order)
    runs = []
    for block in order:
        if runs and runs[-1][1] == block:
            runs[-1][1] = block + 1
        else:
            runs.append([block, block + 1])
    return jnp.concatenate([values[:, a * width : b * width] for a, b in runs], axis=1)


def inverse_of(order):
    inverse = [0] * len(order)
    for place, block in enumerate(order):
        inverse[block] = place
    return inverse


def swapped(values, axis, bit):
    size = lax.axis_size(axis)
    return lax.ppermute(values, axis, [(i, i ^ bit) for i in range(size)])


def gathered_by_doubling(rows, axis):
    size, here = lax.axis_size(axis), lax.axis_index(axis)
    levels = size.bit_length() - 1
    if size != 1 << levels:
        return lax.all_gather(rows, axis, axis=0, tiled=True)
    block = rows.reshape((1,) * levels + rows.shape)
    for place in range(levels):
        bit = 1 << (levels - 1 - place)
        other = swapped(block, axis, bit)
        high = (here & bit) != 0
        block = jnp.concatenate(
            [jnp.where(high, other, block), jnp.where(high, block, other)], axis=place
        )
    return block.reshape((size * rows.shape[0],) + rows.shape[1:])


def scattered_by_halving(total, axis):
    size, here = lax.axis_size(axis), lax.axis_index(axis)
    levels = size.bit_length() - 1
    if size != 1 << levels:
        return lax.psum_scatter(total, axis, scatter_dimension=0, tiled=True)
    rows = total.shape[0] // size
    block = total.reshape((2,) * levels + (rows,) + total.shape[1:])
    for place in range(levels - 1, -1, -1):
        bit = 1 << (levels - 1 - place)
        high = ((here & bit) != 0).astype(jnp.int32)
        kept = lax.dynamic_index_in_dim(block, high, axis=place, keepdims=False)
        sent = lax.dynamic_index_in_dim(block, 1 - high, axis=place, keepdims=False)
        block = kept + swapped(sent.astype(jnp.bfloat16), axis, bit).astype(jnp.float32)
    return block.reshape((rows,) + total.shape[1:])


def carry_kernel(decay_ref, fresh_ref, out_ref, *, reverse):
    count = fresh_ref.shape[0]

    def hop(number, carried):
        k = count - 1 - number if reverse else number
        out_ref[k] = carried.astype(out_ref.dtype)
        return decay_ref[k] * carried + fresh_ref[k].astype(jnp.float32)

    lax.fori_loop(0, count, hop, jnp.zeros(fresh_ref.shape[1:], jnp.float32))


def carried_states(decay_rows, states, axis, reverse):
    size = lax.axis_size(axis)
    share = states.shape[0] // size
    sent = states.astype(jnp.bfloat16).reshape(size, share, states.shape[1])
    fresh = lax.all_to_all(sent, axis, 0, 0, tiled=True)
    folded = pl.pallas_call(
        partial(carry_kernel, reverse=reverse),
        out_shape=jax.ShapeDtypeStruct(fresh.shape, jnp.bfloat16),
        name="carry",
    )(decay_rows, fresh)
    back = lax.all_to_all(folded, axis, 0, 0, tiled=True)
    return back.reshape(states.shape).astype(jnp.float32)


def matmul(left, right):
    return jnp.dot(left, right, preferred_element_type=jnp.float32)


def matmul_tn(left, right):
    return lax.dot_general(
        left, right, (((0,), (0,)), ((), ())), preferred_element_type=jnp.float32
    )


def matmul_nt(left, right):
    return lax.dot_general(
        left, right, (((1,), (1,)), ((), ())), preferred_element_type=jnp.float32
    )


def rms_scale(values):
    return lax.rsqrt(jnp.mean(values * values, axis=-1, keepdims=True) + EPS)


def rms_back(values, inverse, gain_row, upstream):
    scaled = upstream * gain_row
    return inverse * (
        scaled - values * inverse * inverse * jnp.mean(scaled * values, axis=-1, keepdims=True)
    )


def silu_slope(values):
    logistic = jax.nn.sigmoid(values)
    return logistic * (1.0 + values * (1.0 - logistic))


def conv_apply(seg_window, conv_ext, conv_weight, conv_bias):
    out_rows = conv_ext.shape[0] - (KC - 1)
    summed = jnp.broadcast_to(conv_bias[None, :], (out_rows, conv_ext.shape[1]))
    for offset in range(KC):
        same_doc = seg_window[offset : offset + out_rows] == seg_window[KC - 1 :]
        summed = summed + conv_weight[offset][None, :] * jnp.where(
            same_doc[:, None], conv_ext[offset : offset + out_rows], 0.0
        )
    return jax.nn.silu(summed)


def ssm_core(seg_here, seg_before, conv_act, dt_raw, dt_bias, decay_log, skip_gain):
    row_count = conv_act.shape[0]
    blocks_count = row_count // SPAN
    ssm_x = conv_act[:, : HM * HP].reshape(blocks_count, SPAN, HM, HP)
    ssm_b = conv_act[:, HM * HP : HM * HP + NS].reshape(blocks_count, SPAN, NS)
    ssm_c = conv_act[:, HM * HP + NS :].reshape(blocks_count, SPAN, NS)
    step_size = jax.nn.softplus(dt_raw + dt_bias[None, :])
    log_decay = -jnp.exp(decay_log)[None, :] * step_size
    step_heads = step_size.reshape(blocks_count, SPAN, HM).transpose(0, 2, 1)
    cumulative = jnp.cumsum(log_decay.reshape(blocks_count, SPAN, HM).transpose(0, 2, 1), axis=2)
    seg_blocks = seg_here.reshape(blocks_count, SPAN)
    seg_prior = jnp.concatenate([jnp.reshape(seg_before, (1,)), seg_blocks[:-1, -1]])
    seg_last = seg_blocks[:, -1]
    lower = jnp.arange(SPAN)[:, None] >= jnp.arange(SPAN)[None, :]
    visible = (lower[None] & (seg_blocks[:, :, None] == seg_blocks[:, None, :]))[:, None]
    gaps = cumulative[:, :, :, None] - cumulative[:, :, None, :]
    mixing = jnp.where(visible, jnp.exp(jnp.where(visible, gaps, 0.0)), 0.0)
    inner = jnp.einsum("ktn,ksn->kts", ssm_c, ssm_b, precision=HIGH)
    weighted = mixing * inner[:, None] * step_heads[:, :, None, :]
    intra = jnp.einsum("khts,kshp->kthp", weighted, ssm_x, precision=HIGH)
    to_end = (
        jnp.where(
            (seg_blocks == seg_last[:, None])[:, None, :],
            jnp.exp(cumulative[:, :, -1:] - cumulative),
            0.0,
        )
        * step_heads
    )
    block_states = jnp.einsum("khs,kshp,ksn->khpn", to_end, ssm_x, ssm_b, precision=HIGH)
    from_start = jnp.where((seg_blocks == seg_prior[:, None])[:, None, :], jnp.exp(cumulative), 0.0)
    block_decay = from_start[:, :, -1]

    def advance(carried, inputs):
        state_now, product = carried
        decay_now, fresh = inputs
        return (
            (decay_now[:, None, None] * state_now + fresh, product * decay_now),
            (state_now, product),
        )

    initial_carry = (jnp.zeros((HM, HP, NS), jnp.float32), jnp.ones((HM,), jnp.float32))
    (final_state, unused), (entering, products) = lax.scan(
        advance, initial_carry, (block_decay, block_states)
    )
    carried_in = jnp.einsum("kht,ktn,khpn->kthp", from_start, ssm_c, entering, precision=HIGH)
    local_out = (intra + carried_in + skip_gain[None, None, :, None] * ssm_x).reshape(
        row_count, HM, HP
    )
    reach = (from_start * products[:, :, None]).transpose(1, 0, 2).reshape(HM, row_count)
    return (local_out, final_state, reach, ssm_c.reshape(row_count, NS))


def over_keys(update, initial_carry, key_rows_all, row_limit, query_rows, doc_span):
    count_all = key_rows_all.shape[0]
    block_size = math.gcd(count_all, 512)
    blocks = count_all // block_size
    visits = min(blocks, (doc_span + query_rows - 1) // block_size + 2)
    lowest = (row_limit - query_rows - doc_span + 1) // block_size
    begin = jnp.clip(lowest, 0, blocks - visits)

    def visit(number, current_block):
        offset = (begin + number) * block_size
        return update(
            current_block, lax.dynamic_slice_in_dim(key_rows_all, offset, block_size, 0), offset
        )

    return lax.fori_loop(0, visits, visit, initial_carry)


def block_scores(query_quadruple, positions, seg_rows, doc_ids, block_forward_pass, key_start):
    rows_per_block = block_forward_pass.shape[0]
    key_columns = KEYVALUE_HEADS * HEAD_SIZE
    key_row_block = block_forward_pass[:, :key_columns].reshape(
        rows_per_block, KEYVALUE_HEADS, HEAD_SIZE
    )
    value_row_block = block_forward_pass[:, key_columns:].reshape(
        rows_per_block, KEYVALUE_HEADS, HEAD_SIZE
    )
    key_pos = key_start + jnp.arange(rows_per_block, dtype=jnp.int32)
    key_seg = lax.dynamic_slice_in_dim(doc_ids, key_start, rows_per_block)
    visible = (key_pos[None, :] <= positions[:, None]) & (key_seg[None, :] == seg_rows[:, None])
    attention_scores = jnp.einsum(
        "uoiy,woy->oiuw", query_quadruple, key_row_block, preferred_element_type=jnp.float32
    ) * HEAD_SIZE ** (-0.5)
    return (key_row_block, value_row_block, visible[None, None], attention_scores)


def stats_step(
    query_quadruple, positions, seg_rows, doc_ids, denominator, block_forward_pass, key_start
):
    key_row_block, value_row_block, visible, attention_scores = block_scores(
        query_quadruple, positions, seg_rows, doc_ids, block_forward_pass, key_start
    )
    return denominator + jnp.sum(jnp.exp(jnp.where(visible, attention_scores, NEG)), axis=3)


def values_step(
    query_quadruple,
    positions,
    seg_rows,
    doc_ids,
    log_total,
    current_block,
    block_forward_pass,
    key_start,
):
    key_row_block, value_row_block, visible, attention_scores = block_scores(
        query_quadruple, positions, seg_rows, doc_ids, block_forward_pass, key_start
    )
    attention_weights_soft = jnp.exp(
        jnp.where(visible, attention_scores - log_total[..., None], NEG)
    ).astype(jnp.bfloat16)
    return current_block + jnp.einsum(
        "zilr,rzq->lziq",
        attention_weights_soft,
        value_row_block,
        preferred_element_type=jnp.float32,
    )


def back_step(
    query_quadruple,
    positions,
    seg_rows,
    doc_ids,
    log_total,
    gradient_quadruple,
    row_delta,
    current_block,
    block_forward_pass,
    key_start,
):
    query_accumulator, keyvalue_accumulator = current_block
    key_row_block, value_row_block, visible, attention_scores = block_scores(
        query_quadruple, positions, seg_rows, doc_ids, block_forward_pass, key_start
    )
    attention_weights_soft = jnp.exp(
        jnp.where(visible, attention_scores - log_total[..., None], NEG)
    )
    probability_gradient = jnp.einsum(
        "uoiy,woy->oiuw", gradient_quadruple, value_row_block, preferred_element_type=jnp.float32
    )
    score_gradient = (
        attention_weights_soft * (probability_gradient - row_delta[..., None])
    ).astype(jnp.bfloat16)
    query_accumulator = query_accumulator + jnp.einsum(
        "zilr,rzq->lziq", score_gradient, key_row_block, preferred_element_type=jnp.float32
    )
    key_portion = jnp.einsum(
        "luzn,zlup->nlp", score_gradient, query_quadruple, preferred_element_type=jnp.float32
    ) * HEAD_SIZE ** (-0.5)
    value_portion = jnp.einsum(
        "luzn,zlup->nlp",
        attention_weights_soft.astype(jnp.bfloat16),
        gradient_quadruple,
        preferred_element_type=jnp.float32,
    )
    rows_per_block = block_forward_pass.shape[0]
    block_gradient_out = jnp.concatenate(
        [
            key_portion.reshape(rows_per_block, KEYVALUE_HEADS * HEAD_SIZE),
            value_portion.reshape(rows_per_block, KEYVALUE_HEADS * HEAD_SIZE),
        ],
        axis=1,
    )
    old_rows = lax.dynamic_slice_in_dim(keyvalue_accumulator, key_start, rows_per_block, 0)
    keyvalue_accumulator = lax.dynamic_update_slice_in_dim(
        keyvalue_accumulator, old_rows + block_gradient_out, key_start, 0
    )
    return (query_accumulator, keyvalue_accumulator)


def local(
    order,
    layer_input,
    out_grad,
    doc_ids,
    norm1_gain,
    in_weight,
    conv_weight,
    conv_bias,
    dt_bias,
    decay_log,
    skip_gain,
    mixer_out,
    query_weight,
    keyvalue_weight,
    attn_out,
    norm2_gain,
    gate_up,
    down_weight,
):
    local_row_count = layer_input.shape[0]
    devices = lax.axis_size("seq")
    here = lax.axis_index("seq")
    sequence_total = local_row_count * devices
    doc_span = sequence_total // 2 + local_row_count
    first_row = here * local_row_count
    query_group_width = QUERY_HEADS // KEYVALUE_HEADS
    query_cols = QUERY_HEADS * HEAD_SIZE
    keyval_cols = 2 * KEYVALUE_HEADS * HEAD_SIZE
    feature_rows = in_weight.shape[0]
    q_at = DSSM + CONV_CH
    kv_at = q_at + query_cols
    dt_at = kv_at + keyval_cols
    gain_at = dt_at + HM
    packed_cols = -(-(gain_at + 2) // 128) * 128
    first_pack = jnp.concatenate(
        [
            in_weight[:, :q_at],
            query_weight,
            keyvalue_weight,
            in_weight[:, q_at:],
            norm1_gain[:, None],
            norm2_gain[:, None],
            jnp.zeros((feature_rows, packed_cols - gain_at - 2), jnp.bfloat16),
        ],
        axis=1,
    )
    second_pack = jnp.concatenate(
        [gate_up, jnp.concatenate([mixer_out, attn_out, down_weight], axis=0).T], axis=1
    )
    first_full = lax.all_gather(
        first_pack, "seq", axis=0, tiled=True, axis_index_groups=[order]
    )
    second_pack, first_full = lax.optimization_barrier((second_pack, first_full))
    second_full = lax.all_gather(
        second_pack, "seq", axis=0, tiled=True, axis_index_groups=[order]
    )
    gains = first_full[:, gain_at : gain_at + 2].astype(jnp.float32)
    gain_first = gains[:, 0]
    gain_second = gains[:, 1]
    gateup_full = second_full[:, : 2 * FF]
    outward_full = second_full[:, 2 * FF : 2 * FF + DSSM + query_cols]
    downward_full = second_full[:, 2 * FF + DSSM + query_cols :]
    layer_input = reordered(layer_input, order)
    out_grad = reordered(out_grad, order)
    seg_here = lax.dynamic_slice_in_dim(doc_ids, first_row, local_row_count)
    seg_padded = jnp.concatenate([jnp.full((KC - 1,), -1, jnp.int32), doc_ids])
    seg_window = lax.dynamic_slice_in_dim(seg_padded, first_row, local_row_count + KC - 1)
    seg_before = seg_window[KC - 2]
    scale_one = rms_scale(layer_input)
    normed_one = (layer_input * scale_one * gain_first).astype(jnp.bfloat16)
    projected = matmul(normed_one, first_full)
    gate_mix = projected[:, :DSSM]
    conv_in = projected[:, DSSM:q_at]
    query_reduced = projected[:, q_at:kv_at].astype(jnp.bfloat16)
    keyval_low = projected[:, kv_at:dt_at].astype(jnp.bfloat16)
    dt_raw = projected[:, dt_at:gain_at]
    edge_rows = passed_along(conv_in[local_row_count - (KC - 1) :], "seq", 1)
    keyval_all = gathered_by_doubling(keyval_low, "seq")
    conv_ext = jnp.concatenate([edge_rows, conv_in], axis=0)
    conv_act, conv_pull = jax.vjp(partial(conv_apply, seg_window), conv_ext, conv_weight, conv_bias)
    ssm_parts, ssm_pull = jax.vjp(
        partial(ssm_core, seg_here, seg_before), conv_act, dt_raw, dt_bias, decay_log, skip_gain
    )
    local_out, dev_state, reach, c_here = ssm_parts
    dev_decay = reach[:, -1]
    share = HM * HP // devices
    decay_all = gathered_by_doubling(dev_decay[None], "seq")
    decay_rows = lax.dynamic_slice_in_dim(
        jnp.repeat(decay_all, HP, axis=1), here * share, share, 1
    )[:, :, None]
    state_in = carried_states(decay_rows, dev_state.reshape(HM * HP, NS), "seq", False).reshape(
        HM, HP, NS
    )
    cross_base = jnp.einsum("tn,hpn->thp", c_here, state_in, precision=HIGH)
    ssm_out = (local_out + cross_base * reach.T[:, :, None]).reshape(local_row_count, DSSM)
    gated = (ssm_out * jax.nn.silu(gate_mix)).astype(jnp.bfloat16)
    query_quadruple = query_reduced.reshape(
        local_row_count, KEYVALUE_HEADS, query_group_width, HEAD_SIZE
    )
    positions = first_row + jnp.arange(local_row_count, dtype=jnp.int32)
    row_limit = first_row + local_row_count
    statistics_initial = jnp.zeros(
        (KEYVALUE_HEADS, query_group_width, local_row_count), jnp.float32
    )
    middle_initial = jnp.zeros(
        (local_row_count, KEYVALUE_HEADS, query_group_width, HEAD_SIZE), jnp.float32
    )
    stats_update = partial(stats_step, query_quadruple, positions, seg_here, doc_ids)
    denominator = over_keys(
        stats_update, statistics_initial, keyval_all, row_limit, local_row_count, doc_span
    )
    log_total = jnp.log(denominator)
    attention_middle = over_keys(
        partial(values_step, query_quadruple, positions, seg_here, doc_ids, log_total),
        middle_initial,
        keyval_all,
        row_limit,
        local_row_count,
        doc_span,
    )
    attn_low = attention_middle.reshape(local_row_count, query_cols).astype(jnp.bfloat16)
    mixed_low = jnp.concatenate([gated, attn_low], axis=1)
    resid = layer_input + matmul_nt(mixed_low, outward_full)
    scale_two = rms_scale(resid)
    normed_two = (resid * scale_two * gain_second).astype(jnp.bfloat16)
    gateup = matmul(normed_two, gateup_full)
    gate_part = gateup[:, :FF]
    up_part = gateup[:, FF:]
    act_low = (jax.nn.silu(gate_part) * up_part).astype(jnp.bfloat16)
    layer_output = reordered(
        resid + matmul_nt(act_low, downward_full), inverse_of(order)
    )
    grad_low = out_grad.astype(jnp.bfloat16)
    act_grad = matmul(grad_low, downward_full)
    gateup_grad_low = jnp.concatenate(
        [act_grad * up_part * silu_slope(gate_part), act_grad * jax.nn.silu(gate_part)], axis=1
    ).astype(jnp.bfloat16)
    normed_two_grad = matmul_nt(gateup_grad_low, gateup_full)
    gain2_grad = jnp.sum(normed_two_grad * resid * scale_two, axis=0)
    resid_grad = out_grad + rms_back(resid, scale_two, gain_second, normed_two_grad)
    resid_low = resid_grad.astype(jnp.bfloat16)
    second_grad = jnp.concatenate(
        [
            matmul_tn(normed_two, gateup_grad_low).astype(jnp.bfloat16),
            matmul_tn(resid_low, mixed_low).astype(jnp.bfloat16),
            matmul_tn(grad_low, act_low).astype(jnp.bfloat16),
        ],
        axis=1,
    )
    second_share = lax.psum_scatter(
        second_grad, "seq", scatter_dimension=0, tiled=True, axis_index_groups=[order]
    ).astype(jnp.float32)
    mixed_grad = matmul(resid_low, outward_full)
    gated_grad = mixed_grad[:, :DSSM]
    attention_gradient = mixed_grad[:, DSSM:]
    gradient_quadruple = attention_gradient.astype(jnp.bfloat16).reshape(
        local_row_count, KEYVALUE_HEADS, query_group_width, HEAD_SIZE
    )
    row_delta = jnp.sum(
        attention_gradient.reshape(local_row_count, KEYVALUE_HEADS, query_group_width, HEAD_SIZE)
        * attention_middle,
        axis=3,
    ).transpose(1, 2, 0)
    back_init = (
        jnp.zeros((local_row_count, KEYVALUE_HEADS, query_group_width, HEAD_SIZE), jnp.float32),
        jnp.zeros((sequence_total, keyval_cols), jnp.float32),
    )
    back_update = partial(
        back_step,
        query_quadruple,
        positions,
        seg_here,
        doc_ids,
        log_total,
        gradient_quadruple,
        row_delta,
    )
    query_accumulator, keyvalue_accumulator = over_keys(
        back_update, back_init, keyval_all, row_limit, local_row_count, doc_span
    )
    keyval_here = scattered_by_halving(keyvalue_accumulator, "seq")
    query_grad_low = (
        query_accumulator.reshape(local_row_count, query_cols) * HEAD_SIZE ** (-0.5)
    ).astype(jnp.bfloat16)
    keyval_grad_low = keyval_here.astype(jnp.bfloat16)
    ssm_grad = gated_grad * jax.nn.silu(gate_mix)
    gate_mix_grad = gated_grad * ssm_out * silu_slope(gate_mix)
    ssm_grad_three = ssm_grad.reshape(local_row_count, HM, HP)
    weighted_grad = ssm_grad_three * reach.T[:, :, None]
    state_in_grad = jnp.einsum("thp,tn->hpn", weighted_grad, c_here, precision=HIGH)
    c_grad = jnp.einsum("thp,hpn->tn", weighted_grad, state_in, precision=HIGH)
    reach_grad = jnp.einsum("thp,thp->ht", ssm_grad_three, cross_base, precision=HIGH)
    state_out_grad = carried_states(
        decay_rows, state_in_grad.reshape(HM * HP, NS), "seq", True
    ).reshape(HM, HP, NS)
    decay_grad = jnp.sum(state_out_grad * state_in, axis=(1, 2))
    reach_grad = jnp.concatenate(
        [reach_grad[:, :-1], reach_grad[:, -1:] + decay_grad[:, None]], axis=1
    )
    act_grad_ssm, dt_raw_grad, dt_bias_grad, decay_log_grad, skip_grad = ssm_pull(
        (ssm_grad_three, state_out_grad, reach_grad, c_grad)
    )
    ext_grad, conv_weight_grad, conv_bias_grad = conv_pull(act_grad_ssm)
    edge_back = passed_along(ext_grad[: KC - 1], "seq", -1)
    conv_in_grad = ext_grad[KC - 1 :] + jnp.concatenate(
        [jnp.zeros((local_row_count - (KC - 1), CONV_CH), jnp.float32), edge_back], axis=0
    )
    first_grad_low = jnp.concatenate(
        [
            gate_mix_grad.astype(jnp.bfloat16),
            conv_in_grad.astype(jnp.bfloat16),
            query_grad_low,
            keyval_grad_low,
            dt_raw_grad.astype(jnp.bfloat16),
            jnp.zeros((local_row_count, packed_cols - gain_at), jnp.bfloat16),
        ],
        axis=1,
    )
    first_share = lax.psum_scatter(
        matmul_tn(normed_one, first_grad_low).astype(jnp.bfloat16),
        "seq",
        scatter_dimension=0,
        tiled=True,
        axis_index_groups=[order],
    ).astype(jnp.float32)
    normed_one_grad = matmul_nt(first_grad_low, first_full)
    gain1_grad = jnp.sum(normed_one_grad * layer_input * scale_one, axis=0)
    input_grad = reordered(
        resid_grad + rms_back(layer_input, scale_one, gain_first, normed_one_grad),
        inverse_of(order),
    )
    small = (
        conv_weight_grad,
        conv_bias_grad,
        dt_bias_grad,
        decay_log_grad,
        skip_grad,
        gain1_grad,
        gain2_grad,
    )
    flat = lax.psum(jnp.concatenate([part.reshape(-1) for part in small]), "seq")
    sums, at = ([], 0)
    for part in small:
        sums.append(flat[at : at + part.size].reshape(part.shape))
        at += part.size
    place = jnp.asarray(inverse_of(order), jnp.int32)[here] * feature_rows
    mixed_at = 2 * FF
    down_at = mixed_at + DSSM + query_cols
    return (
        layer_output,
        input_grad,
        lax.dynamic_slice_in_dim(sums[5], place, feature_rows),
        jnp.concatenate([first_share[:, :q_at], first_share[:, dt_at:gain_at]], axis=1),
        sums[0],
        sums[1],
        sums[2],
        sums[3],
        sums[4],
        second_share[:, mixed_at : mixed_at + DSSM].T,
        first_share[:, q_at:kv_at],
        first_share[:, kv_at:dt_at],
        second_share[:, mixed_at + DSSM : down_at].T,
        lax.dynamic_slice_in_dim(sums[6], place, feature_rows),
        second_share[:, :mixed_at],
        second_share[:, down_at:].T,
    )


def solution(mesh):
    placed = (
        P("seq", None),
        P("seq", None),
        P(),
        P("seq"),
        P("seq", None),
        P(),
        P(),
        P(),
        P(),
        P(),
        P(None, "seq"),
        P("seq", None),
        P("seq", None),
        P(None, "seq"),
        P("seq"),
        P("seq", None),
        P(None, "seq"),
    )
    return jax.shard_map(
        partial(local, ring_order(mesh.shape["seq"])),
        mesh=mesh,
        in_specs=placed,
        out_specs=(
            P("seq", None),
            P("seq", None),
            P("seq"),
            P("seq", None),
            P(),
            P(),
            P(),
            P(),
            P(),
            P(None, "seq"),
            P("seq", None),
            P("seq", None),
            P(None, "seq"),
            P("seq"),
            P("seq", None),
            P(None, "seq"),
        ),
        check_vma=False,
    )
```

```python
from functools import partial
import math

import jax
import jax.numpy as jnp
from jax import lax
from jax.experimental import pallas as pl
from jax.experimental.pallas import tpu as pltpu
from jax.sharding import PartitionSpec as P

FF = 2048
HM = 24
HP = 64
NS = 128
KC = 4
QUERY_HEADS = 8
KEYVALUE_HEADS = 2
HEAD_SIZE = 64
SPAN = 128
DSSM = 1536
CONV_CH = 1792


EPS = 1e-05
HIGH = lax.Precision.HIGHEST
NEG = -1e30


def passed_along(block, axis, distance):
    devices = range(lax.axis_size(axis))
    route = [(i - distance, i) for i in devices if i - distance in devices]
    return lax.ppermute(block, axis, route)


def ring_order(devices):
    chips = devices // 2
    depth = 4
    side = math.isqrt(max(chips // depth, 1))
    if devices % 2 or chips != depth * side * side or side % 2:
        return list(range(devices))
    plane = []
    for a in range(side):
        line = [(a, b) for b in range(1, side)]
        plane += line if a % 2 == 0 else line[::-1]
    plane += [(a, 0) for a in range(side - 1, -1, -1)]
    order = []
    for number, (a, b) in enumerate(plane):
        levels = range(depth) if number % 2 == 0 else range(depth - 1, -1, -1)
        for z in levels:
            chip = (z * side + a) * side + b
            order += [2 * chip, 2 * chip + 1]
    return order


def reordered(values, order):
    width = values.shape[1] // len(order)
    runs = []
    for block in order:
        if runs and runs[-1][1] == block:
            runs[-1][1] = block + 1
        else:
            runs.append([block, block + 1])
    return jnp.concatenate([values[:, a * width : b * width] for a, b in runs], axis=1)


def inverse_of(order):
    inverse = [0] * len(order)
    for place, block in enumerate(order):
        inverse[block] = place
    return inverse


def swapped(values, axis, bit):
    size = lax.axis_size(axis)
    return lax.ppermute(values, axis, [(i, i ^ bit) for i in range(size)])


def gathered_by_doubling(rows, axis):
    size, here = lax.axis_size(axis), lax.axis_index(axis)
    levels = size.bit_length() - 1
    if size != 1 << levels:
        return lax.all_gather(rows, axis, axis=0, tiled=True)
    block = rows.reshape((1,) * levels + rows.shape)
    for place in range(levels):
        bit = 1 << (levels - 1 - place)
        other = swapped(block, axis, bit)
        high = (here & bit) != 0
        block = jnp.concatenate(
            [jnp.where(high, other, block), jnp.where(high, block, other)], axis=place
        )
    return block.reshape((size * rows.shape[0],) + rows.shape[1:])


def scattered_by_halving(total, axis):
    size, here = lax.axis_size(axis), lax.axis_index(axis)
    levels = size.bit_length() - 1
    if size != 1 << levels:
        return lax.psum_scatter(total, axis, scatter_dimension=0, tiled=True)
    rows = total.shape[0] // size
    block = total.reshape((2,) * levels + (rows,) + total.shape[1:])
    for place in range(levels - 1, -1, -1):
        bit = 1 << (levels - 1 - place)
        high = ((here & bit) != 0).astype(jnp.int32)
        kept = lax.dynamic_index_in_dim(block, high, axis=place, keepdims=False)
        sent = lax.dynamic_index_in_dim(block, 1 - high, axis=place, keepdims=False)
        block = kept.astype(jnp.float32) + swapped(sent.astype(jnp.bfloat16), axis, bit).astype(
            jnp.float32
        )
    return block.reshape((rows,) + total.shape[1:])


def carry_kernel(decay_ref, fresh_ref, out_ref, *, reverse):
    count = fresh_ref.shape[0]

    def hop(number, carried):
        k = count - 1 - number if reverse else number
        out_ref[k] = carried.astype(out_ref.dtype)
        return decay_ref[k] * carried + fresh_ref[k].astype(jnp.float32)

    lax.fori_loop(0, count, hop, jnp.zeros(fresh_ref.shape[1:], jnp.float32))


def carried_states(decay_rows, states, axis, reverse):
    size = lax.axis_size(axis)
    share = states.shape[0] // size
    sent = states.astype(jnp.bfloat16).reshape(size, share, states.shape[1])
    fresh = lax.all_to_all(sent, axis, 0, 0, tiled=True)
    folded = pl.pallas_call(
        partial(carry_kernel, reverse=reverse),
        out_shape=jax.ShapeDtypeStruct(fresh.shape, jnp.bfloat16),
        name="carry",
    )(decay_rows, fresh)
    back = lax.all_to_all(folded, axis, 0, 0, tiled=True)
    return back.reshape(states.shape).astype(jnp.float32)


def matmul(left, right):
    return jnp.dot(left, right, preferred_element_type=jnp.float32)


def matmul_tn(left, right):
    return lax.dot_general(
        left, right, (((0,), (0,)), ((), ())), preferred_element_type=jnp.float32
    )


def matmul_nt(left, right):
    return lax.dot_general(
        left, right, (((1,), (1,)), ((), ())), preferred_element_type=jnp.float32
    )


def rms_scale(values):
    return lax.rsqrt(jnp.mean(values * values, axis=-1, keepdims=True) + EPS)


def rms_back(values, inverse, gain_row, upstream):
    scaled = upstream * gain_row
    return inverse * (
        scaled - values * inverse * inverse * jnp.mean(scaled * values, axis=-1, keepdims=True)
    )


def silu_slope(values):
    logistic = jax.nn.sigmoid(values)
    return logistic * (1.0 + values * (1.0 - logistic))


def conv_apply(seg_window, conv_ext, conv_weight, conv_bias):
    out_rows = conv_ext.shape[0] - (KC - 1)
    summed = jnp.broadcast_to(conv_bias[None, :], (out_rows, conv_ext.shape[1]))
    for offset in range(KC):
        same_doc = seg_window[offset : offset + out_rows] == seg_window[KC - 1 :]
        summed = summed + conv_weight[offset][None, :] * jnp.where(
            same_doc[:, None], conv_ext[offset : offset + out_rows], 0.0
        )
    return jax.nn.silu(summed)


def ssm_core(seg_here, seg_before, conv_act, dt_raw, dt_bias, decay_log, skip_gain):
    row_count = conv_act.shape[0]
    blocks_count = row_count // SPAN
    ssm_x = conv_act[:, : HM * HP].reshape(blocks_count, SPAN, HM, HP)
    ssm_b = conv_act[:, HM * HP : HM * HP + NS].reshape(blocks_count, SPAN, NS)
    ssm_c = conv_act[:, HM * HP + NS :].reshape(blocks_count, SPAN, NS)
    step_size = jax.nn.softplus(dt_raw + dt_bias[None, :])
    log_decay = -jnp.exp(decay_log)[None, :] * step_size
    step_heads = step_size.reshape(blocks_count, SPAN, HM).transpose(0, 2, 1)
    cumulative = jnp.cumsum(log_decay.reshape(blocks_count, SPAN, HM).transpose(0, 2, 1), axis=2)
    seg_blocks = seg_here.reshape(blocks_count, SPAN)
    seg_prior = jnp.concatenate([jnp.reshape(seg_before, (1,)), seg_blocks[:-1, -1]])
    seg_last = seg_blocks[:, -1]
    lower = jnp.arange(SPAN)[:, None] >= jnp.arange(SPAN)[None, :]
    visible = (lower[None] & (seg_blocks[:, :, None] == seg_blocks[:, None, :]))[:, None]
    gaps = cumulative[:, :, :, None] - cumulative[:, :, None, :]
    mixing = jnp.where(visible, jnp.exp(jnp.where(visible, gaps, 0.0)), 0.0)
    inner = jnp.einsum("ktn,ksn->kts", ssm_c, ssm_b, precision=HIGH)
    weighted = mixing * inner[:, None] * step_heads[:, :, None, :]
    intra = jnp.einsum("khts,kshp->kthp", weighted, ssm_x, precision=HIGH)
    to_end = (
        jnp.where(
            (seg_blocks == seg_last[:, None])[:, None, :],
            jnp.exp(cumulative[:, :, -1:] - cumulative),
            0.0,
        )
        * step_heads
    )
    block_states = jnp.einsum("khs,kshp,ksn->khpn", to_end, ssm_x, ssm_b, precision=HIGH)
    from_start = jnp.where((seg_blocks == seg_prior[:, None])[:, None, :], jnp.exp(cumulative), 0.0)
    block_decay = from_start[:, :, -1]

    def advance(carried, inputs):
        state_now, product = carried
        decay_now, fresh = inputs
        return (
            (decay_now[:, None, None] * state_now + fresh, product * decay_now),
            (state_now, product),
        )

    initial_carry = (jnp.zeros((HM, HP, NS), jnp.float32), jnp.ones((HM,), jnp.float32))
    (final_state, unused), (entering, products) = lax.scan(
        advance, initial_carry, (block_decay, block_states)
    )
    carried_in = jnp.einsum("kht,ktn,khpn->kthp", from_start, ssm_c, entering, precision=HIGH)
    local_out = (intra + carried_in + skip_gain[None, None, :, None] * ssm_x).reshape(
        row_count, HM, HP
    )
    reach = (from_start * products[:, :, None]).transpose(1, 0, 2).reshape(HM, row_count)
    return (local_out, final_state, reach, ssm_c.reshape(row_count, NS))


def stacked_heads(values, kv):
    group = QUERY_HEADS // KEYVALUE_HEADS
    heads = range(kv * group, (kv + 1) * group)
    return jnp.concatenate([values[:, h * HEAD_SIZE : (h + 1) * HEAD_SIZE] for h in heads], axis=0)


def visible_pairs(number, block, first_row, seg_rows, seg_all_ref, rows):
    group = QUERY_HEADS // KEYVALUE_HEADS
    row_pos = first_row + lax.broadcasted_iota(jnp.int32, (rows, block), 0)
    key_pos = number * block + lax.broadcasted_iota(jnp.int32, (rows, block), 1)
    visible = (key_pos <= row_pos) & (seg_all_ref[pl.ds(number, 1), :] == seg_rows)
    bias = jnp.where(visible, 0.0, NEG)
    return jnp.concatenate([bias] * group, axis=0)


def attention_forward_kernel(
    bounds_ref, query_ref, keyval_ref, seg_row_ref, seg_all_ref, out_ref, total_ref
):
    rows, block = (seg_row_ref.shape[0], seg_all_ref.shape[1])
    height = rows * (QUERY_HEADS // KEYVALUE_HEADS)
    queries = [stacked_heads(query_ref[...], kv) for kv in range(KEYVALUE_HEADS)]
    seg_rows = seg_row_ref[...]

    def visit(number, carried):
        at = pl.multiple_of(number * block, block)
        bias = visible_pairs(number, block, bounds_ref[2], seg_rows, seg_all_ref, rows)
        keyval = keyval_ref[pl.ds(at, block), :]
        new = []
        for kv in range(KEYVALUE_HEADS):
            most, total, mixed = carried[kv]
            key = keyval[:, kv * HEAD_SIZE : (kv + 1) * HEAD_SIZE]
            value_at = (KEYVALUE_HEADS + kv) * HEAD_SIZE
            value = keyval[:, value_at : value_at + HEAD_SIZE]
            scores = matmul_nt(queries[kv], key) * HEAD_SIZE ** (-0.5) + bias
            new_most = jnp.maximum(most, jnp.max(scores, axis=1, keepdims=True))
            shrink = jnp.exp(most - new_most)
            weights = jnp.exp(scores - new_most)
            total = total * shrink + jnp.sum(weights, axis=1, keepdims=True)
            mixed = mixed * shrink + matmul(weights.astype(jnp.bfloat16), value)
            new.append((new_most, total, mixed))
        return tuple(new)

    start = (
        jnp.full((height, 1), NEG, jnp.float32),
        jnp.zeros((height, 1), jnp.float32),
        jnp.zeros((height, HEAD_SIZE), jnp.float32),
    )
    done = lax.fori_loop(bounds_ref[0], bounds_ref[1], visit, (start,) * KEYVALUE_HEADS)
    for kv in range(KEYVALUE_HEADS):
        most, total, mixed = done[kv]
        mixed = mixed / total
        total_ref[kv] = most + jnp.log(total)
        for g in range(height // rows):
            at = (kv * (height // rows) + g) * HEAD_SIZE
            out_ref[:, at : at + HEAD_SIZE] = mixed[g * rows : (g + 1) * rows]


def attention_backward_kernel(
    bounds_ref,
    query_ref,
    keyval_ref,
    seg_row_ref,
    seg_all_ref,
    total_ref,
    mid_ref,
    grad_ref,
    query_grad_ref,
    keyval_grad_ref,
):
    rows, block = (seg_row_ref.shape[0], seg_all_ref.shape[1])
    height = rows * (QUERY_HEADS // KEYVALUE_HEADS)
    heads = range(KEYVALUE_HEADS)
    queries = [stacked_heads(query_ref[...], kv) for kv in heads]
    grads = [stacked_heads(grad_ref[...], kv) for kv in heads]
    deltas = [
        jnp.sum(grads[kv] * stacked_heads(mid_ref[...], kv), axis=1, keepdims=True) for kv in heads
    ]
    grads = [part.astype(jnp.bfloat16) for part in grads]
    totals = [total_ref[kv] for kv in heads]
    seg_rows = seg_row_ref[...]
    keyval_grad_ref[...] = jnp.zeros(keyval_grad_ref.shape, keyval_grad_ref.dtype)

    def visit(number, carried):
        at = pl.multiple_of(number * block, block)
        bias = visible_pairs(number, block, bounds_ref[2], seg_rows, seg_all_ref, rows)
        keyval = keyval_ref[pl.ds(at, block), :]
        new = []
        for kv in heads:
            key = keyval[:, kv * HEAD_SIZE : (kv + 1) * HEAD_SIZE]
            value_at = (KEYVALUE_HEADS + kv) * HEAD_SIZE
            value = keyval[:, value_at : value_at + HEAD_SIZE]
            scores = matmul_nt(queries[kv], key) * HEAD_SIZE ** (-0.5) + bias
            weights = jnp.exp(scores - totals[kv])
            score_grad = (weights * (matmul_nt(grads[kv], value) - deltas[kv])).astype(jnp.bfloat16)
            new.append(carried[kv] + matmul(score_grad, key))
            key_grad = matmul_tn(score_grad, queries[kv]) * HEAD_SIZE ** (-0.5)
            value_grad = matmul_tn(weights.astype(jnp.bfloat16), grads[kv])
            low = keyval_grad_ref.dtype
            keyval_grad_ref[pl.ds(at, block), kv * HEAD_SIZE : (kv + 1) * HEAD_SIZE] = (
                key_grad.astype(low)
            )
            keyval_grad_ref[pl.ds(at, block), value_at : value_at + HEAD_SIZE] = value_grad.astype(
                low
            )
        return tuple(new)

    start = jnp.zeros((height, HEAD_SIZE), jnp.float32)
    done = lax.fori_loop(bounds_ref[0], bounds_ref[1], visit, (start,) * KEYVALUE_HEADS)
    for kv in heads:
        for g in range(height // rows):
            at = (kv * (height // rows) + g) * HEAD_SIZE
            query_grad_ref[:, at : at + HEAD_SIZE] = (
                done[kv][g * rows : (g + 1) * rows] * HEAD_SIZE ** (-0.5)
            ).astype(query_grad_ref.dtype)


def in_smem():
    return pl.BlockSpec(memory_space=pltpu.SMEM)


def in_vmem():
    return pl.BlockSpec(memory_space=pltpu.VMEM)


def attention_forward(bounds, query, keyval_all, seg_rows, seg_all):
    rows = query.shape[0]
    height = rows * (QUERY_HEADS // KEYVALUE_HEADS)
    return pl.pallas_call(
        attention_forward_kernel,
        in_specs=[in_smem()] + [in_vmem()] * 4,
        out_shape=(
            jax.ShapeDtypeStruct(query.shape, jnp.float32),
            jax.ShapeDtypeStruct((KEYVALUE_HEADS, height, 1), jnp.float32),
        ),
        name="attend",
    )(bounds, query, keyval_all, seg_rows, seg_all)


def attention_backward(bounds, query, keyval_all, seg_rows, seg_all, totals, mid, grad):
    return pl.pallas_call(
        attention_backward_kernel,
        in_specs=[in_smem()] + [in_vmem()] * 7,
        out_shape=(
            jax.ShapeDtypeStruct(query.shape, jnp.bfloat16),
            jax.ShapeDtypeStruct(keyval_all.shape, jnp.bfloat16),
        ),
        name="attend_back",
    )(bounds, query, keyval_all, seg_rows, seg_all, totals, mid, grad)


def local(
    order,
    layer_input,
    out_grad,
    doc_ids,
    norm1_gain,
    in_weight,
    conv_weight,
    conv_bias,
    dt_bias,
    decay_log,
    skip_gain,
    mixer_out,
    query_weight,
    keyvalue_weight,
    attn_out,
    norm2_gain,
    gate_up,
    down_weight,
):
    local_row_count = layer_input.shape[0]
    devices = lax.axis_size("seq")
    here = lax.axis_index("seq")
    sequence_total = local_row_count * devices
    first_row = here * local_row_count
    query_cols = QUERY_HEADS * HEAD_SIZE
    keyval_cols = 2 * KEYVALUE_HEADS * HEAD_SIZE
    feature_rows = in_weight.shape[0]
    q_at = DSSM + CONV_CH
    kv_at = q_at + query_cols
    dt_at = kv_at + keyval_cols
    gain_at = dt_at + HM
    packed_cols = -(-(gain_at + 2) // 128) * 128
    first_pack = jnp.concatenate(
        [
            in_weight[:, :q_at],
            query_weight,
            keyvalue_weight,
            in_weight[:, q_at:],
            norm1_gain[:, None],
            norm2_gain[:, None],
            jnp.zeros((feature_rows, packed_cols - gain_at - 2), jnp.bfloat16),
        ],
        axis=1,
    )
    second_pack = jnp.concatenate(
        [gate_up, jnp.concatenate([mixer_out, attn_out, down_weight], axis=0).T], axis=1
    )
    first_full = lax.all_gather(
        first_pack, "seq", axis=0, tiled=True, axis_index_groups=[order]
    )
    second_pack, first_full = lax.optimization_barrier((second_pack, first_full))
    second_full = lax.all_gather(
        second_pack, "seq", axis=0, tiled=True, axis_index_groups=[order]
    )
    gains = first_full[:, gain_at : gain_at + 2].astype(jnp.float32)
    gain_first = gains[:, 0]
    gain_second = gains[:, 1]
    gateup_full = second_full[:, : 2 * FF]
    outward_full = second_full[:, 2 * FF : 2 * FF + DSSM + query_cols]
    downward_full = second_full[:, 2 * FF + DSSM + query_cols :]
    layer_input = reordered(layer_input, order)
    out_grad = reordered(out_grad, order)
    seg_here = lax.dynamic_slice_in_dim(doc_ids, first_row, local_row_count)
    seg_padded = jnp.concatenate([jnp.full((KC - 1,), -1, jnp.int32), doc_ids])
    seg_window = lax.dynamic_slice_in_dim(seg_padded, first_row, local_row_count + KC - 1)
    seg_before = seg_window[KC - 2]
    scale_one = rms_scale(layer_input)
    normed_one = (layer_input * scale_one * gain_first).astype(jnp.bfloat16)
    projected = matmul(normed_one, first_full)
    gate_mix = projected[:, :DSSM]
    conv_in = projected[:, DSSM:q_at]
    query_reduced = projected[:, q_at:kv_at].astype(jnp.bfloat16)
    keyval_low = projected[:, kv_at:dt_at].astype(jnp.bfloat16)
    dt_raw = projected[:, dt_at:gain_at]
    edge_rows = passed_along(conv_in[local_row_count - (KC - 1) :], "seq", 1)
    keyval_all = gathered_by_doubling(keyval_low, "seq")
    conv_ext = jnp.concatenate([edge_rows, conv_in], axis=0)
    conv_act, conv_pull = jax.vjp(partial(conv_apply, seg_window), conv_ext, conv_weight, conv_bias)
    ssm_parts, ssm_pull = jax.vjp(
        partial(ssm_core, seg_here, seg_before), conv_act, dt_raw, dt_bias, decay_log, skip_gain
    )
    local_out, dev_state, reach, c_here = ssm_parts
    dev_decay = reach[:, -1]
    share = HM * HP // devices
    decay_all = gathered_by_doubling(dev_decay[None], "seq")
    decay_rows = lax.dynamic_slice_in_dim(
        jnp.repeat(decay_all, HP, axis=1), here * share, share, 1
    )[:, :, None]
    state_in = carried_states(decay_rows, dev_state.reshape(HM * HP, NS), "seq", False).reshape(
        HM, HP, NS
    )
    cross_base = jnp.einsum("tn,hpn->thp", c_here, state_in, precision=HIGH)
    ssm_out = (local_out + cross_base * reach.T[:, :, None]).reshape(local_row_count, DSSM)
    gated = (ssm_out * jax.nn.silu(gate_mix)).astype(jnp.bfloat16)
    key_block = math.gcd(sequence_total, 256)
    first_key = jnp.sum((doc_ids < seg_here[0]).astype(jnp.int32))
    bounds = jnp.stack(
        [first_key // key_block, (first_row + local_row_count - 1) // key_block + 1, first_row]
    ).astype(jnp.int32)
    seg_column = seg_here[:, None]
    seg_all = doc_ids.reshape(sequence_total // key_block, key_block)
    attention_middle, log_total = attention_forward(
        bounds, query_reduced, keyval_all, seg_column, seg_all
    )
    attn_low = attention_middle.astype(jnp.bfloat16)
    mixed_low = jnp.concatenate([gated, attn_low], axis=1)
    resid = layer_input + matmul_nt(mixed_low, outward_full)
    scale_two = rms_scale(resid)
    normed_two = (resid * scale_two * gain_second).astype(jnp.bfloat16)
    gateup = matmul(normed_two, gateup_full)
    gate_part = gateup[:, :FF]
    up_part = gateup[:, FF:]
    act_low = (jax.nn.silu(gate_part) * up_part).astype(jnp.bfloat16)
    layer_output = reordered(
        resid + matmul_nt(act_low, downward_full), inverse_of(order)
    )
    grad_low = out_grad.astype(jnp.bfloat16)
    act_grad = matmul(grad_low, downward_full)
    gateup_grad_low = jnp.concatenate(
        [act_grad * up_part * silu_slope(gate_part), act_grad * jax.nn.silu(gate_part)], axis=1
    ).astype(jnp.bfloat16)
    normed_two_grad = matmul_nt(gateup_grad_low, gateup_full)
    gain2_grad = jnp.sum(normed_two_grad * resid * scale_two, axis=0)
    resid_grad = out_grad + rms_back(resid, scale_two, gain_second, normed_two_grad)
    resid_low = resid_grad.astype(jnp.bfloat16)
    second_grad = jnp.concatenate(
        [
            matmul_tn(normed_two, gateup_grad_low).astype(jnp.bfloat16),
            matmul_tn(resid_low, mixed_low).astype(jnp.bfloat16),
            matmul_tn(grad_low, act_low).astype(jnp.bfloat16),
        ],
        axis=1,
    )
    mixed_grad = matmul(resid_low, outward_full)
    second_grad, mixed_grad = lax.optimization_barrier((second_grad, mixed_grad))
    second_share = lax.psum_scatter(
        second_grad, "seq", scatter_dimension=0, tiled=True, axis_index_groups=[order]
    ).astype(jnp.float32)
    gated_grad = mixed_grad[:, :DSSM]
    query_grad_low, keyval_partial = attention_backward(
        bounds,
        query_reduced,
        keyval_all,
        seg_column,
        seg_all,
        log_total,
        attention_middle,
        mixed_grad[:, DSSM:],
    )
    keyval_grad_low = scattered_by_halving(keyval_partial, "seq").astype(jnp.bfloat16)
    ssm_grad = gated_grad * jax.nn.silu(gate_mix)
    gate_mix_grad = gated_grad * ssm_out * silu_slope(gate_mix)
    ssm_grad_three = ssm_grad.reshape(local_row_count, HM, HP)
    weighted_grad = ssm_grad_three * reach.T[:, :, None]
    state_in_grad = jnp.einsum("thp,tn->hpn", weighted_grad, c_here, precision=HIGH)
    c_grad = jnp.einsum("thp,hpn->tn", weighted_grad, state_in, precision=HIGH)
    reach_grad = jnp.einsum("thp,thp->ht", ssm_grad_three, cross_base, precision=HIGH)
    state_out_grad = carried_states(
        decay_rows, state_in_grad.reshape(HM * HP, NS), "seq", True
    ).reshape(HM, HP, NS)
    decay_grad = jnp.sum(state_out_grad * state_in, axis=(1, 2))
    reach_grad = jnp.concatenate(
        [reach_grad[:, :-1], reach_grad[:, -1:] + decay_grad[:, None]], axis=1
    )
    act_grad_ssm, dt_raw_grad, dt_bias_grad, decay_log_grad, skip_grad = ssm_pull(
        (ssm_grad_three, state_out_grad, reach_grad, c_grad)
    )
    ext_grad, conv_weight_grad, conv_bias_grad = conv_pull(act_grad_ssm)
    edge_back = passed_along(ext_grad[: KC - 1], "seq", -1)
    conv_in_grad = ext_grad[KC - 1 :] + jnp.concatenate(
        [jnp.zeros((local_row_count - (KC - 1), CONV_CH), jnp.float32), edge_back], axis=0
    )
    first_grad_low = jnp.concatenate(
        [
            gate_mix_grad.astype(jnp.bfloat16),
            conv_in_grad.astype(jnp.bfloat16),
            query_grad_low,
            keyval_grad_low,
            dt_raw_grad.astype(jnp.bfloat16),
            jnp.zeros((local_row_count, packed_cols - gain_at), jnp.bfloat16),
        ],
        axis=1,
    )
    first_share = lax.psum_scatter(
        matmul_tn(normed_one, first_grad_low).astype(jnp.bfloat16),
        "seq",
        scatter_dimension=0,
        tiled=True,
        axis_index_groups=[order],
    ).astype(jnp.float32)
    normed_one_grad = matmul_nt(first_grad_low, first_full)
    gain1_grad = jnp.sum(normed_one_grad * layer_input * scale_one, axis=0)
    input_grad = reordered(
        resid_grad + rms_back(layer_input, scale_one, gain_first, normed_one_grad),
        inverse_of(order),
    )
    small = (
        conv_weight_grad,
        conv_bias_grad,
        dt_bias_grad,
        decay_log_grad,
        skip_grad,
        gain1_grad,
        gain2_grad,
    )
    flat = lax.psum(jnp.concatenate([part.reshape(-1) for part in small]), "seq")
    sums, at = ([], 0)
    for part in small:
        sums.append(flat[at : at + part.size].reshape(part.shape))
        at += part.size
    place = jnp.asarray(inverse_of(order), jnp.int32)[here] * feature_rows
    mixed_at = 2 * FF
    down_at = mixed_at + DSSM + query_cols
    return (
        layer_output,
        input_grad,
        lax.dynamic_slice_in_dim(sums[5], place, feature_rows),
        jnp.concatenate([first_share[:, :q_at], first_share[:, dt_at:gain_at]], axis=1),
        sums[0],
        sums[1],
        sums[2],
        sums[3],
        sums[4],
        second_share[:, mixed_at : mixed_at + DSSM].T,
        first_share[:, q_at:kv_at],
        first_share[:, kv_at:dt_at],
        second_share[:, mixed_at + DSSM : down_at].T,
        lax.dynamic_slice_in_dim(sums[6], place, feature_rows),
        second_share[:, :mixed_at],
        second_share[:, down_at:].T,
    )


def solution(mesh):
    placed = (
        P("seq", None),
        P("seq", None),
        P(),
        P("seq"),
        P("seq", None),
        P(),
        P(),
        P(),
        P(),
        P(),
        P(None, "seq"),
        P("seq", None),
        P("seq", None),
        P(None, "seq"),
        P("seq"),
        P("seq", None),
        P(None, "seq"),
    )
    return jax.shard_map(
        partial(local, ring_order(mesh.shape["seq"])),
        mesh=mesh,
        in_specs=placed,
        out_specs=(
            P("seq", None),
            P("seq", None),
            P("seq"),
            P("seq", None),
            P(),
            P(),
            P(),
            P(),
            P(),
            P(None, "seq"),
            P("seq", None),
            P("seq", None),
            P(None, "seq"),
            P("seq"),
            P("seq", None),
            P(None, "seq"),
        ),
        check_vma=False,
    )
```

```python
from functools import partial
import math

import jax
import jax.numpy as jnp
from jax import lax
from jax.experimental import pallas as pl
from jax.experimental.pallas import tpu as pltpu
from jax.sharding import PartitionSpec as P

FF = 2048
HM = 24
HP = 64
NS = 128
KC = 4
QUERY_HEADS = 8
KEYVALUE_HEADS = 2
HEAD_SIZE = 64
DSSM = 1536
CONV_CH = 1792


EPS = 1e-05
HIGH = lax.Precision.HIGHEST
NEG = -1e30


def passed_along(block, axis, distance):
    devices = range(lax.axis_size(axis))
    route = [(i - distance, i) for i in devices if i - distance in devices]
    return lax.ppermute(block, axis, route)


def ring_order(devices):
    chips = devices // 2
    depth = 4
    side = math.isqrt(max(chips // depth, 1))
    if devices % 2 or chips != depth * side * side or side % 2:
        return list(range(devices))
    plane = []
    for a in range(side):
        line = [(a, b) for b in range(1, side)]
        plane += line if a % 2 == 0 else line[::-1]
    plane += [(a, 0) for a in range(side - 1, -1, -1)]
    order = []
    for number, (a, b) in enumerate(plane):
        levels = range(depth) if number % 2 == 0 else range(depth - 1, -1, -1)
        for z in levels:
            chip = (z * side + a) * side + b
            order += [2 * chip, 2 * chip + 1]
    return order


def reordered(values, order):
    width = values.shape[1] // len(order)
    runs = []
    for block in order:
        if runs and runs[-1][1] == block:
            runs[-1][1] = block + 1
        else:
            runs.append([block, block + 1])
    return jnp.concatenate([values[:, a * width : b * width] for a, b in runs], axis=1)


def inverse_of(order):
    inverse = [0] * len(order)
    for place, block in enumerate(order):
        inverse[block] = place
    return inverse


def swapped(values, axis, bit):
    size = lax.axis_size(axis)
    return lax.ppermute(values, axis, [(i, i ^ bit) for i in range(size)])


def gathered_by_doubling(rows, axis):
    size, here = lax.axis_size(axis), lax.axis_index(axis)
    levels = size.bit_length() - 1
    if size != 1 << levels:
        return lax.all_gather(rows, axis, axis=0, tiled=True)
    block = rows.reshape((1,) * levels + rows.shape)
    for place in range(levels):
        bit = 1 << (levels - 1 - place)
        other = swapped(block, axis, bit)
        high = (here & bit) != 0
        block = jnp.concatenate(
            [jnp.where(high, other, block), jnp.where(high, block, other)], axis=place
        )
    return block.reshape((size * rows.shape[0],) + rows.shape[1:])


def scattered_by_halving(total, axis):
    size, here = lax.axis_size(axis), lax.axis_index(axis)
    levels = size.bit_length() - 1
    if size != 1 << levels:
        return lax.psum_scatter(total, axis, scatter_dimension=0, tiled=True)
    rows = total.shape[0] // size
    block = total.reshape((2,) * levels + (rows,) + total.shape[1:])
    for place in range(levels - 1, -1, -1):
        bit = 1 << (levels - 1 - place)
        high = ((here & bit) != 0).astype(jnp.int32)
        kept = lax.dynamic_index_in_dim(block, high, axis=place, keepdims=False)
        sent = lax.dynamic_index_in_dim(block, 1 - high, axis=place, keepdims=False)
        block = kept.astype(jnp.float32) + swapped(sent.astype(jnp.bfloat16), axis, bit).astype(
            jnp.float32
        )
    return block.reshape((rows,) + total.shape[1:])


def carry_kernel(decay_ref, fresh_ref, out_ref, *, reverse):
    count = fresh_ref.shape[0]

    def hop(number, carried):
        k = count - 1 - number if reverse else number
        out_ref[k] = carried.astype(out_ref.dtype)
        return decay_ref[k] * carried + fresh_ref[k].astype(jnp.float32)

    lax.fori_loop(0, count, hop, jnp.zeros(fresh_ref.shape[1:], jnp.float32))


def carried_states(decay_rows, states, axis, reverse):
    size = lax.axis_size(axis)
    share = states.shape[0] // size
    sent = states.reshape(size, share, states.shape[1])
    fresh = lax.all_to_all(sent, axis, 0, 0, tiled=True)
    folded = pl.pallas_call(
        partial(carry_kernel, reverse=reverse),
        out_shape=jax.ShapeDtypeStruct(fresh.shape, jnp.bfloat16),
        name="carry",
    )(decay_rows, fresh)
    back = lax.all_to_all(folded, axis, 0, 0, tiled=True)
    return back.reshape(states.shape)


def matmul(left, right):
    return jnp.dot(left, right, preferred_element_type=jnp.float32)


def matmul_tn(left, right):
    return lax.dot_general(
        left, right, (((0,), (0,)), ((), ())), preferred_element_type=jnp.float32
    )


def matmul_nt(left, right):
    return lax.dot_general(
        left, right, (((1,), (1,)), ((), ())), preferred_element_type=jnp.float32
    )


def rms_scale(values):
    return lax.rsqrt(jnp.mean(values * values, axis=-1, keepdims=True) + EPS)


def rms_back(values, inverse, gain_row, upstream):
    scaled = upstream * gain_row
    return inverse * (
        scaled - values * inverse * inverse * jnp.mean(scaled * values, axis=-1, keepdims=True)
    )


def silu_slope(values):
    logistic = jax.nn.sigmoid(values)
    return logistic * (1.0 + values * (1.0 - logistic))


def stacked_heads(values, kv):
    group = QUERY_HEADS // KEYVALUE_HEADS
    heads = range(kv * group, (kv + 1) * group)
    return jnp.concatenate([values[:, h * HEAD_SIZE : (h + 1) * HEAD_SIZE] for h in heads], axis=0)


def visible_pairs(number, block, first_row, seg_rows, seg_all_ref, rows):
    group = QUERY_HEADS // KEYVALUE_HEADS
    row_pos = first_row + lax.broadcasted_iota(jnp.int32, (rows, block), 0)
    key_pos = number * block + lax.broadcasted_iota(jnp.int32, (rows, block), 1)
    visible = (key_pos <= row_pos) & (seg_all_ref[pl.ds(number, 1), :] == seg_rows)
    bias = jnp.where(visible, 0.0, NEG)
    return jnp.concatenate([bias] * group, axis=0)


def attention_forward_kernel(
    bounds_ref, query_ref, keyval_ref, seg_row_ref, seg_all_ref, out_ref, total_ref
):
    rows, block = (seg_row_ref.shape[0], seg_all_ref.shape[1])
    height = rows * (QUERY_HEADS // KEYVALUE_HEADS)
    queries = [stacked_heads(query_ref[...], kv) for kv in range(KEYVALUE_HEADS)]
    seg_rows = seg_row_ref[...]

    def visit(number, carried):
        at = pl.multiple_of(number * block, block)
        bias = visible_pairs(number, block, bounds_ref[2], seg_rows, seg_all_ref, rows)
        keyval = keyval_ref[pl.ds(at, block), :]
        new = []
        for kv in range(KEYVALUE_HEADS):
            most, total, mixed = carried[kv]
            key = keyval[:, kv * HEAD_SIZE : (kv + 1) * HEAD_SIZE]
            value_at = (KEYVALUE_HEADS + kv) * HEAD_SIZE
            value = keyval[:, value_at : value_at + HEAD_SIZE]
            scores = matmul_nt(queries[kv], key) * HEAD_SIZE ** (-0.5) + bias
            new_most = jnp.maximum(most, jnp.max(scores, axis=1, keepdims=True))
            shrink = jnp.exp(most - new_most)
            weights = jnp.exp(scores - new_most)
            total = total * shrink + jnp.sum(weights, axis=1, keepdims=True)
            mixed = mixed * shrink + matmul(weights.astype(jnp.bfloat16), value)
            new.append((new_most, total, mixed))
        return tuple(new)

    start = (
        jnp.full((height, 1), NEG, jnp.float32),
        jnp.zeros((height, 1), jnp.float32),
        jnp.zeros((height, HEAD_SIZE), jnp.float32),
    )
    done = lax.fori_loop(bounds_ref[0], bounds_ref[1], visit, (start,) * KEYVALUE_HEADS)
    for kv in range(KEYVALUE_HEADS):
        most, total, mixed = done[kv]
        mixed = mixed / total
        total_ref[kv] = most + jnp.log(total)
        for g in range(height // rows):
            at = (kv * (height // rows) + g) * HEAD_SIZE
            out_ref[:, at : at + HEAD_SIZE] = mixed[g * rows : (g + 1) * rows]


def attention_backward_kernel(
    bounds_ref,
    query_ref,
    keyval_ref,
    seg_row_ref,
    seg_all_ref,
    total_ref,
    mid_ref,
    grad_ref,
    query_grad_ref,
    keyval_grad_ref,
):
    rows, block = (seg_row_ref.shape[0], seg_all_ref.shape[1])
    height = rows * (QUERY_HEADS // KEYVALUE_HEADS)
    heads = range(KEYVALUE_HEADS)
    queries = [stacked_heads(query_ref[...], kv) for kv in heads]
    grads = [stacked_heads(grad_ref[...], kv) for kv in heads]
    deltas = [
        jnp.sum(grads[kv] * stacked_heads(mid_ref[...], kv), axis=1, keepdims=True) for kv in heads
    ]
    grads = [part.astype(jnp.bfloat16) for part in grads]
    totals = [total_ref[kv] for kv in heads]
    seg_rows = seg_row_ref[...]
    keyval_grad_ref[...] = jnp.zeros(keyval_grad_ref.shape, keyval_grad_ref.dtype)

    def visit(number, carried):
        at = pl.multiple_of(number * block, block)
        bias = visible_pairs(number, block, bounds_ref[2], seg_rows, seg_all_ref, rows)
        keyval = keyval_ref[pl.ds(at, block), :]
        new = []
        for kv in heads:
            key = keyval[:, kv * HEAD_SIZE : (kv + 1) * HEAD_SIZE]
            value_at = (KEYVALUE_HEADS + kv) * HEAD_SIZE
            value = keyval[:, value_at : value_at + HEAD_SIZE]
            scores = matmul_nt(queries[kv], key) * HEAD_SIZE ** (-0.5) + bias
            weights = jnp.exp(scores - totals[kv])
            score_grad = (weights * (matmul_nt(grads[kv], value) - deltas[kv])).astype(jnp.bfloat16)
            new.append(carried[kv] + matmul(score_grad, key))
            key_grad = matmul_tn(score_grad, queries[kv]) * HEAD_SIZE ** (-0.5)
            value_grad = matmul_tn(weights.astype(jnp.bfloat16), grads[kv])
            low = keyval_grad_ref.dtype
            keyval_grad_ref[pl.ds(at, block), kv * HEAD_SIZE : (kv + 1) * HEAD_SIZE] = (
                key_grad.astype(low)
            )
            keyval_grad_ref[pl.ds(at, block), value_at : value_at + HEAD_SIZE] = value_grad.astype(
                low
            )
        return tuple(new)

    start = jnp.zeros((height, HEAD_SIZE), jnp.float32)
    done = lax.fori_loop(bounds_ref[0], bounds_ref[1], visit, (start,) * KEYVALUE_HEADS)
    for kv in heads:
        for g in range(height // rows):
            at = (kv * (height // rows) + g) * HEAD_SIZE
            query_grad_ref[:, at : at + HEAD_SIZE] = (
                done[kv][g * rows : (g + 1) * rows] * HEAD_SIZE ** (-0.5)
            ).astype(query_grad_ref.dtype)


def in_smem():
    return pl.BlockSpec(memory_space=pltpu.SMEM)


def in_vmem():
    return pl.BlockSpec(memory_space=pltpu.VMEM)


def attention_forward(bounds, query, keyval_all, seg_rows, seg_all):
    rows = query.shape[0]
    height = rows * (QUERY_HEADS // KEYVALUE_HEADS)
    return pl.pallas_call(
        attention_forward_kernel,
        in_specs=[in_smem()] + [in_vmem()] * 4,
        out_shape=(
            jax.ShapeDtypeStruct(query.shape, jnp.float32),
            jax.ShapeDtypeStruct((KEYVALUE_HEADS, height, 1), jnp.float32),
        ),
        name="attend",
    )(bounds, query, keyval_all, seg_rows, seg_all)


def attention_backward(bounds, query, keyval_all, seg_rows, seg_all, totals, mid, grad):
    return pl.pallas_call(
        attention_backward_kernel,
        in_specs=[in_smem()] + [in_vmem()] * 7,
        out_shape=(
            jax.ShapeDtypeStruct(query.shape, jnp.bfloat16),
            jax.ShapeDtypeStruct(keyval_all.shape, jnp.bfloat16),
        ),
        name="attend_back",
    )(bounds, query, keyval_all, seg_rows, seg_all, totals, mid, grad)


EDGE = 8


def dot_exact(left, right, contract):
    return lax.dot_general(
        left, right, (contract, ((), ())), precision=HIGH, preferred_element_type=jnp.float32
    )


def low(values):
    return values.astype(jnp.bfloat16)


def head_columns(width):
    head = lax.broadcasted_iota(jnp.int32, (HM, width), 0)
    channel = lax.broadcasted_iota(jnp.int32, (HM, width), 1)
    return ((channel >= head * HP) & (channel < (head + 1) * HP)).astype(jnp.float32)


def to_channels(per_head):
    return dot_exact(per_head, head_columns(DSSM), ((1,), (0,)))


def to_heads(per_channel):
    return dot_exact(per_channel, head_columns(DSSM), ((1,), (1,)))


def silu_of(values):
    return values * jax.nn.sigmoid(values)


def softplus_of(values):
    return jnp.maximum(values, 0.0) + jnp.log1p(jnp.exp(-jnp.abs(values)))


class Decays:
    def __init__(self, dt_raw, dt_bias, decay_log, seg_column, seg_row, seg_before):
        rows = dt_raw.shape[0]
        at = lax.broadcasted_iota(jnp.int32, (rows, rows), 0)
        to = lax.broadcasted_iota(jnp.int32, (rows, rows), 1)
        self.lower = (at >= to).astype(jnp.float32)
        self.same = (at == to).astype(jnp.float32)
        self.shifted = dt_raw + dt_bias
        self.step = softplus_of(self.shifted)
        self.rate = -jnp.exp(decay_log)
        self.log_decay = self.rate * self.step
        self.total = dot_exact(self.lower, self.log_decay, ((1,), (0,)))
        self.total_lanes = dot_exact(self.total, self.same, ((0,), (0,)))
        self.step_lanes = dot_exact(self.step, self.same, ((0,), (0,)))
        self.bias = jnp.where((at >= to) & (seg_column == seg_row), 0.0, NEG)
        last = lax.broadcasted_iota(jnp.int32, (rows, HM), 0) == rows - 1
        self.last = last.astype(jnp.float32)
        end = jnp.sum(self.last * self.total, axis=0, keepdims=True)
        to_last = seg_column == seg_column[rows - 1 :, :]
        self.end_only = jnp.where(to_last, jnp.exp(jnp.where(to_last, end - self.total, 0.0)), 0.0)
        self.to_end = self.end_only * self.step
        self.reach = jnp.where(seg_column == seg_before, jnp.exp(self.total), 0.0)

    def mixing(self, h):
        gap = self.total[:, h : h + 1] - self.total_lanes[h : h + 1, :]
        return jnp.exp(gap + self.bias)


def conv_pieces(pre_ref):
    act = silu_of(pre_ref[...])
    return (act[:, :DSSM], act[:, DSSM : DSSM + NS], act[:, DSSM + NS :])


def in_half(values, second):
    lane = lax.broadcasted_iota(jnp.int32, values.shape, 1)
    return jnp.where((lane >= HP) == second, values, jnp.zeros_like(values))


def ssm_forward_kernel(
    seg_before_ref,
    projected_ref,
    edge_ref,
    same_ref,
    seg_column_ref,
    seg_row_ref,
    conv_weight_ref,
    conv_bias_ref,
    dt_bias_ref,
    decay_log_ref,
    skip_ref,
    pre_ref,
    local_ref,
    state_ref,
    reach_ref,
    ext_ref,
    *,
    dt_at,
):
    rows = projected_ref.shape[0]
    ext_ref[:EDGE] = edge_ref[...]
    ext_ref[EDGE:] = projected_ref[:, DSSM : DSSM + CONV_CH]
    pre = jnp.broadcast_to(conv_bias_ref[...], (rows, CONV_CH))
    for k in range(KC):
        at = EDGE - (KC - 1) + k
        pre = pre + conv_weight_ref[k : k + 1, :] * (
            same_ref[:, k : k + 1] * ext_ref[at : at + rows, :]
        )
    pre_ref[...] = pre
    ssm_x, ssm_b, ssm_c = conv_pieces(pre_ref)
    decays = Decays(
        projected_ref[:, dt_at : dt_at + HM],
        dt_bias_ref[...],
        decay_log_ref[...],
        seg_column_ref[...],
        seg_row_ref[...],
        seg_before_ref[0],
    )
    inner = dot_exact(ssm_c, ssm_b, ((1,), (1,)))
    x_low = low(ssm_x)
    skip = to_channels(jnp.broadcast_to(skip_ref[...], (EDGE, HM)))[:1]
    for pair in range(HM // 2):
        at = pair * 2 * HP
        x_pair = x_low[:, at : at + 2 * HP]
        parts = []
        for h in (2 * pair, 2 * pair + 1):
            weighted = decays.mixing(h) * inner * decays.step_lanes[h : h + 1, :]
            parts.append(in_half(matmul(low(weighted), x_pair), h % 2 == 1))
        local_ref[:, at : at + 2 * HP] = (
            parts[0] + parts[1] + skip[:, at : at + 2 * HP] * ssm_x[:, at : at + 2 * HP]
        )
    state_ref[...] = low(matmul_tn(low(ssm_x * to_channels(decays.to_end)), low(ssm_b)))
    reach_ref[...] = decays.reach


def ssm_join_kernel(projected_ref, local_ref, pre_ref, state_ref, reach_ref, out_ref, gated_ref):
    ssm_c = silu_of(pre_ref[:, DSSM + NS :])
    crossed = matmul_nt(low(ssm_c), state_ref[...])
    out = local_ref[...] + crossed * to_channels(reach_ref[...])
    out_ref[...] = out
    gated_ref[...] = low(out * silu_of(projected_ref[:, :DSSM]))


def ssm_gate_back_kernel(
    projected_ref, mixed_grad_ref, out_ref, pre_ref, reach_ref, gate_grad_ref, grad_ref, state_ref
):
    gate = projected_ref[:, :DSSM]
    gated_grad = mixed_grad_ref[:, :DSSM]
    grad = gated_grad * silu_of(gate)
    grad_ref[...] = grad
    gate_grad_ref[...] = low(gated_grad * out_ref[...] * silu_slope(gate))
    ssm_c = silu_of(pre_ref[:, DSSM + NS :])
    state_ref[...] = low(matmul_tn(low(grad * to_channels(reach_ref[...])), low(ssm_c)))


def ssm_backward_kernel(
    seg_before_ref,
    projected_ref,
    edge_ref,
    same_ref,
    seg_column_ref,
    seg_row_ref,
    conv_weight_ref,
    dt_bias_ref,
    decay_log_ref,
    skip_ref,
    pre_ref,
    grad_ref,
    state_in_ref,
    state_grad_ref,
    conv_in_grad_ref,
    edge_grad_ref,
    dt_grad_ref,
    conv_weight_grad_ref,
    conv_bias_grad_ref,
    head_grad_ref,
    ext_ref,
    act_grad_ref,
    *,
    dt_at,
):
    rows = projected_ref.shape[0]
    ssm_x, ssm_b, ssm_c = conv_pieces(pre_ref)
    decays = Decays(
        projected_ref[:, dt_at : dt_at + HM],
        dt_bias_ref[...],
        decay_log_ref[...],
        seg_column_ref[...],
        seg_row_ref[...],
        seg_before_ref[0],
    )
    inner = dot_exact(ssm_c, ssm_b, ((1,), (1,)))
    grad = grad_ref[...]
    x_low, grad_low, b_low, c_low = (low(ssm_x), low(grad), low(ssm_b), low(ssm_c))
    skip = to_channels(jnp.broadcast_to(skip_ref[...], (EDGE, HM)))[:1]
    to_end_wide = to_channels(decays.to_end)
    state_in, state_grad = (state_in_ref[...], state_grad_ref[...])
    from_state = matmul_nt(b_low, state_grad)
    head_lane = lax.broadcasted_iota(jnp.int32, (rows, HM), 1)
    head_row = lax.broadcasted_iota(jnp.int32, (HM, rows), 0)
    row_sums = jnp.zeros((rows, HM), jnp.float32)
    step_grad_lanes = jnp.zeros((HM, rows), jnp.float32)
    inner_grad = jnp.zeros((rows, rows), jnp.float32)
    for pair in range(HM // 2):
        at = pair * 2 * HP
        x_pair = x_low[:, at : at + 2 * HP]
        x_grad = skip[:, at : at + 2 * HP] * grad[:, at : at + 2 * HP]
        x_grad = x_grad + to_end_wide[:, at : at + 2 * HP] * from_state[:, at : at + 2 * HP]
        for h in (2 * pair, 2 * pair + 1):
            out_grad = in_half(grad_low[:, at : at + 2 * HP], h % 2 == 1)
            mixing = decays.mixing(h)
            steps = decays.step_lanes[h : h + 1, :]
            weighted = mixing * inner * steps
            weight_grad = matmul_nt(out_grad, x_pair) * mixing
            inner_grad = inner_grad + weight_grad * steps
            step_part = weight_grad * inner
            step_grad_lanes = jnp.where(
                head_row == h, jnp.sum(step_part, axis=0, keepdims=True), step_grad_lanes
            )
            row_sums = jnp.where(
                head_lane == h, jnp.sum(step_part * steps, axis=1, keepdims=True), row_sums
            )
            x_grad = x_grad + matmul_tn(low(weighted), out_grad)
        act_grad_ref[:, at : at + 2 * HP] = x_grad
    inner_low = low(inner_grad)
    act_grad_ref[:, DSSM : DSSM + NS] = matmul(low(ssm_x * to_end_wide), state_grad) + matmul_tn(
        inner_low, c_low
    )
    act_grad_ref[:, DSSM + NS :] = matmul(
        low(grad * to_channels(decays.reach)), state_in
    ) + matmul(inner_low, b_low)
    crossed = matmul_nt(c_low, state_in)
    products = state_in.astype(jnp.float32) * state_grad.astype(jnp.float32)
    carried = dot_exact(jnp.ones((EDGE, NS), jnp.float32), products, ((1,), (1,)))
    decay_grad = to_heads(carried)[:1]
    reach_grad = to_heads(grad * crossed) + decays.last * decay_grad
    end_grad = to_heads(ssm_x * from_state)
    end_part = end_grad * decays.to_end
    step_columns = dot_exact(decays.same, step_grad_lanes, ((1,), (1,)))
    total_grad = (
        row_sums
        - step_columns * decays.step
        + reach_grad * decays.reach
        - end_part
        + decays.last * jnp.sum(end_part, axis=0, keepdims=True)
    )
    log_grad = dot_exact(decays.lower, total_grad, ((0,), (0,)))
    step_grad = step_columns + end_grad * decays.end_only + log_grad * decays.rate
    dt_grad = step_grad * jax.nn.sigmoid(decays.shifted)
    dt_grad_ref[...] = dt_grad
    head_grad_ref[0:1, :] = jnp.sum(dt_grad, axis=0, keepdims=True)
    head_grad_ref[1:2, :] = jnp.sum(log_grad * decays.log_decay, axis=0, keepdims=True)
    head_grad_ref[2:3, :] = jnp.sum(to_heads(grad * ssm_x), axis=0, keepdims=True)
    pre_grad = act_grad_ref[...] * silu_slope(pre_ref[...])
    conv_bias_grad_ref[...] = jnp.sum(pre_grad, axis=0, keepdims=True)
    ext_ref[:EDGE] = edge_ref[...]
    ext_ref[EDGE:] = projected_ref[:, DSSM : DSSM + CONV_CH]
    parts = []
    for k in range(KC):
        at = EDGE - (KC - 1) + k
        masked = pre_grad * same_ref[:, k : k + 1]
        conv_weight_grad_ref[k : k + 1, :] = jnp.sum(
            masked * ext_ref[at : at + rows, :], axis=0, keepdims=True
        )
        parts.append(masked * conv_weight_ref[k : k + 1, :])
    ext_ref[...] = jnp.zeros(ext_ref.shape, jnp.float32)
    for k in range(KC):
        at = EDGE - (KC - 1) + k
        ext_ref[at : at + rows, :] = ext_ref[at : at + rows, :] + parts[k]
    edge_grad_ref[...] = ext_ref[:EDGE]
    conv_in_grad_ref[...] = ext_ref[EDGE:]


def of(shape, kind=jnp.float32):
    return jax.ShapeDtypeStruct(shape, kind)


def ssm_forward(dt_at, *operands):
    rows = operands[1].shape[0]
    return pl.pallas_call(
        partial(ssm_forward_kernel, dt_at=dt_at),
        in_specs=[in_smem()] + [in_vmem()] * 10,
        out_shape=(
            of((rows, CONV_CH)),
            of((rows, DSSM)),
            of((DSSM, NS), jnp.bfloat16),
            of((rows, HM)),
        ),
        scratch_shapes=[pltpu.VMEM((rows + EDGE, CONV_CH), jnp.float32)],
        name="ssm_forward",
    )(*operands)


def ssm_join(projected, *operands):
    rows = projected.shape[0]
    return pl.pallas_call(
        ssm_join_kernel,
        in_specs=[in_vmem()] * 5,
        out_shape=(of((rows, DSSM)), of((rows, DSSM), jnp.bfloat16)),
        name="ssm_join",
    )(projected, *operands)


def ssm_gate_back(projected, *operands):
    rows = projected.shape[0]
    return pl.pallas_call(
        ssm_gate_back_kernel,
        in_specs=[in_vmem()] * 5,
        out_shape=(
            of((rows, DSSM), jnp.bfloat16),
            of((rows, DSSM)),
            of((DSSM, NS), jnp.bfloat16),
        ),
        name="ssm_gate_back",
    )(projected, *operands)


def ssm_backward(dt_at, *operands):
    rows = operands[1].shape[0]
    return pl.pallas_call(
        partial(ssm_backward_kernel, dt_at=dt_at),
        in_specs=[in_smem()] + [in_vmem()] * 13,
        out_shape=(
            of((rows, CONV_CH)),
            of((EDGE, CONV_CH)),
            of((rows, HM)),
            of((KC, CONV_CH)),
            of((1, CONV_CH)),
            of((3, HM)),
        ),
        scratch_shapes=[
            pltpu.VMEM((rows + EDGE, CONV_CH), jnp.float32),
            pltpu.VMEM((rows, CONV_CH), jnp.float32),
        ],
        name="ssm_backward",
    )(*operands)


def local(
    order,
    layer_input,
    out_grad,
    doc_ids,
    norm1_gain,
    in_weight,
    conv_weight,
    conv_bias,
    dt_bias,
    decay_log,
    skip_gain,
    mixer_out,
    query_weight,
    keyvalue_weight,
    attn_out,
    norm2_gain,
    gate_up,
    down_weight,
):
    local_row_count = layer_input.shape[0]
    devices = lax.axis_size("seq")
    here = lax.axis_index("seq")
    sequence_total = local_row_count * devices
    first_row = here * local_row_count
    query_cols = QUERY_HEADS * HEAD_SIZE
    keyval_cols = 2 * KEYVALUE_HEADS * HEAD_SIZE
    feature_rows = in_weight.shape[0]
    q_at = DSSM + CONV_CH
    kv_at = q_at + query_cols
    dt_at = kv_at + keyval_cols
    gain_at = dt_at + HM
    packed_cols = -(-(gain_at + 2) // 128) * 128
    first_pack = jnp.concatenate(
        [
            in_weight[:, :q_at],
            query_weight,
            keyvalue_weight,
            in_weight[:, q_at:],
            norm1_gain[:, None],
            norm2_gain[:, None],
            jnp.zeros((feature_rows, packed_cols - gain_at - 2), jnp.bfloat16),
        ],
        axis=1,
    )
    second_pack = jnp.concatenate(
        [gate_up, jnp.concatenate([mixer_out, attn_out, down_weight], axis=0).T], axis=1
    )
    first_full = lax.all_gather(
        first_pack, "seq", axis=0, tiled=True, axis_index_groups=[order]
    )
    second_pack, first_full = lax.optimization_barrier((second_pack, first_full))
    second_full = lax.all_gather(
        second_pack, "seq", axis=0, tiled=True, axis_index_groups=[order]
    )
    gains = first_full[:, gain_at : gain_at + 2].astype(jnp.float32)
    gain_first = gains[:, 0]
    gain_second = gains[:, 1]
    gateup_full = second_full[:, : 2 * FF]
    outward_full = second_full[:, 2 * FF : 2 * FF + DSSM + query_cols]
    downward_full = second_full[:, 2 * FF + DSSM + query_cols :]
    layer_input = reordered(layer_input, order)
    out_grad = reordered(out_grad, order)
    seg_here = lax.dynamic_slice_in_dim(doc_ids, first_row, local_row_count)
    seg_padded = jnp.concatenate([jnp.full((KC - 1,), -1, jnp.int32), doc_ids])
    seg_window = lax.dynamic_slice_in_dim(seg_padded, first_row, local_row_count + KC - 1)
    seg_before = seg_window[KC - 2]
    scale_one = rms_scale(layer_input)
    normed_one = (layer_input * scale_one * gain_first).astype(jnp.bfloat16)
    projected = matmul(normed_one, first_full)
    query_reduced = projected[:, q_at:kv_at].astype(jnp.bfloat16)
    keyval_low = projected[:, kv_at:dt_at].astype(jnp.bfloat16)
    edge_rows = passed_along(projected[local_row_count - EDGE :, DSSM:q_at], "seq", 1)
    keyval_all = gathered_by_doubling(keyval_low, "seq")
    seg_column = seg_here[:, None]
    same_doc = jnp.stack(
        [
            (seg_window[k : k + local_row_count] == seg_here).astype(jnp.float32)
            for k in range(KC)
        ],
        axis=1,
    )
    step_sum = jnp.sum(jax.nn.softplus(projected[:, dt_at:gain_at] + dt_bias[None, :]), axis=0)
    dev_decay = jnp.where(
        seg_here[local_row_count - 1] == seg_before, jnp.exp(-jnp.exp(decay_log) * step_sum), 0.0
    )
    share = DSSM // devices
    decay_all = gathered_by_doubling(dev_decay[None], "seq")
    decay_rows = lax.dynamic_slice_in_dim(
        jnp.repeat(decay_all, HP, axis=1), here * share, share, 1
    )[:, :, None]
    placing = (
        seg_before[None],
        projected,
        edge_rows,
        same_doc,
        seg_column,
        seg_here[None, :],
        conv_weight,
    )
    head_rows = (dt_bias[None, :], decay_log[None, :], skip_gain[None, :])
    conv_pre, local_out, dev_state, reach = ssm_forward(
        dt_at, *placing, conv_bias[None, :], *head_rows
    )
    state_in = carried_states(decay_rows, dev_state, "seq", False)
    ssm_out, gated = ssm_join(projected, local_out, conv_pre, state_in, reach)
    key_block = math.gcd(sequence_total, 256)
    first_key = jnp.sum((doc_ids < seg_here[0]).astype(jnp.int32))
    bounds = jnp.stack(
        [first_key // key_block, (first_row + local_row_count - 1) // key_block + 1, first_row]
    ).astype(jnp.int32)
    seg_all = doc_ids.reshape(sequence_total // key_block, key_block)
    attention_middle, log_total = attention_forward(
        bounds, query_reduced, keyval_all, seg_column, seg_all
    )
    attn_low = attention_middle.astype(jnp.bfloat16)
    mixed_low = jnp.concatenate([gated, attn_low], axis=1)
    resid = layer_input + matmul_nt(mixed_low, outward_full)
    scale_two = rms_scale(resid)
    normed_two = (resid * scale_two * gain_second).astype(jnp.bfloat16)
    gateup = matmul(normed_two, gateup_full)
    gate_part = gateup[:, :FF]
    up_part = gateup[:, FF:]
    act_low = (jax.nn.silu(gate_part) * up_part).astype(jnp.bfloat16)
    layer_output = reordered(
        resid + matmul_nt(act_low, downward_full), inverse_of(order)
    )
    grad_low = out_grad.astype(jnp.bfloat16)
    act_grad = matmul(grad_low, downward_full)
    gateup_grad_low = jnp.concatenate(
        [act_grad * up_part * silu_slope(gate_part), act_grad * jax.nn.silu(gate_part)], axis=1
    ).astype(jnp.bfloat16)
    normed_two_grad = matmul_nt(gateup_grad_low, gateup_full)
    gain2_grad = jnp.sum(normed_two_grad * resid * scale_two, axis=0)
    resid_grad = out_grad + rms_back(resid, scale_two, gain_second, normed_two_grad)
    resid_low = resid_grad.astype(jnp.bfloat16)
    second_grad = jnp.concatenate(
        [
            matmul_tn(normed_two, gateup_grad_low).astype(jnp.bfloat16),
            matmul_tn(resid_low, mixed_low).astype(jnp.bfloat16),
            matmul_tn(grad_low, act_low).astype(jnp.bfloat16),
        ],
        axis=1,
    )
    mixed_grad = matmul(resid_low, outward_full)
    second_grad, mixed_grad = lax.optimization_barrier((second_grad, mixed_grad))
    second_share = lax.psum_scatter(
        second_grad, "seq", scatter_dimension=0, tiled=True, axis_index_groups=[order]
    )
    gate_mix_grad, ssm_grad, state_in_grad = ssm_gate_back(
        projected, mixed_grad, ssm_out, conv_pre, reach
    )
    state_out_grad = carried_states(decay_rows, state_in_grad, "seq", True)
    query_grad_low, keyval_partial = attention_backward(
        bounds,
        query_reduced,
        keyval_all,
        seg_column,
        seg_all,
        log_total,
        attention_middle,
        mixed_grad[:, DSSM:],
    )
    keyval_grad_low = scattered_by_halving(keyval_partial, "seq").astype(jnp.bfloat16)
    conv_own_grad, edge_grad, dt_raw_grad, conv_weight_grad, conv_bias_grad, head_grad = (
        ssm_backward(dt_at, *placing, *head_rows, conv_pre, ssm_grad, state_in, state_out_grad)
    )
    edge_back = passed_along(edge_grad, "seq", -1)
    conv_in_grad = jnp.concatenate(
        [
            conv_own_grad[: local_row_count - EDGE],
            conv_own_grad[local_row_count - EDGE :] + edge_back,
        ],
        axis=0,
    )
    first_grad_low = jnp.concatenate(
        [
            gate_mix_grad,
            conv_in_grad.astype(jnp.bfloat16),
            query_grad_low,
            keyval_grad_low,
            dt_raw_grad.astype(jnp.bfloat16),
            jnp.zeros((local_row_count, packed_cols - gain_at), jnp.bfloat16),
        ],
        axis=1,
    )
    first_grad = matmul_tn(normed_one, first_grad_low).astype(jnp.bfloat16)
    first_grad, second_share = lax.optimization_barrier((first_grad, second_share))
    first_share = lax.psum_scatter(
        first_grad, "seq", scatter_dimension=0, tiled=True, axis_index_groups=[order]
    ).astype(jnp.float32)
    second_share = second_share.astype(jnp.float32)
    normed_one_grad = matmul_nt(first_grad_low, first_full)
    gain1_grad = jnp.sum(normed_one_grad * layer_input * scale_one, axis=0)
    input_grad = reordered(
        resid_grad + rms_back(layer_input, scale_one, gain_first, normed_one_grad),
        inverse_of(order),
    )
    small = (
        conv_weight_grad,
        conv_bias_grad[0],
        head_grad[0],
        head_grad[1],
        head_grad[2],
        gain1_grad,
        gain2_grad,
    )
    flat = lax.psum(jnp.concatenate([part.reshape(-1) for part in small]), "seq")
    sums, at = ([], 0)
    for part in small:
        sums.append(flat[at : at + part.size].reshape(part.shape))
        at += part.size
    place = jnp.asarray(inverse_of(order), jnp.int32)[here] * feature_rows
    mixed_at = 2 * FF
    down_at = mixed_at + DSSM + query_cols
    return (
        layer_output,
        input_grad,
        lax.dynamic_slice_in_dim(sums[5], place, feature_rows),
        jnp.concatenate([first_share[:, :q_at], first_share[:, dt_at:gain_at]], axis=1),
        sums[0],
        sums[1],
        sums[2],
        sums[3],
        sums[4],
        second_share[:, mixed_at : mixed_at + DSSM].T,
        first_share[:, q_at:kv_at],
        first_share[:, kv_at:dt_at],
        second_share[:, mixed_at + DSSM : down_at].T,
        lax.dynamic_slice_in_dim(sums[6], place, feature_rows),
        second_share[:, :mixed_at],
        second_share[:, down_at:].T,
    )


def solution(mesh):
    placed = (
        P("seq", None),
        P("seq", None),
        P(),
        P("seq"),
        P("seq", None),
        P(),
        P(),
        P(),
        P(),
        P(),
        P(None, "seq"),
        P("seq", None),
        P("seq", None),
        P(None, "seq"),
        P("seq"),
        P("seq", None),
        P(None, "seq"),
    )
    return jax.shard_map(
        partial(local, ring_order(mesh.shape["seq"])),
        mesh=mesh,
        in_specs=placed,
        out_specs=(
            P("seq", None),
            P("seq", None),
            P("seq"),
            P("seq", None),
            P(),
            P(),
            P(),
            P(),
            P(),
            P(None, "seq"),
            P("seq", None),
            P("seq", None),
            P(None, "seq"),
            P("seq"),
            P("seq", None),
            P(None, "seq"),
        ),
        check_vma=False,
    )
```
